256 devices in a mesh: row: 8 (over z_hi, core), col: 4 (over x), cfg: 8 (over y, z_lo).
Axes of the slice: x: 4, y: 4, z: 8 (z_hi: 4, z_lo: 2; z = z_hi * 2 + z_lo), core: 2. Of those that a mesh axis runs over, the one named last changes fastest.
Arguments:
- eigvec: bfloat16 [18432, 18432], P('row', ('col', 'cfg')), may hold values from -0.046875 to 0.046875
- force_const: bfloat16 [18432, 18432], P(('col', 'cfg'), 'row'), may hold values from -0.046875 to 0.046875
- amplitudes: bfloat16 [18432, 1024], P(('col', 'cfg')), may hold values from -6 to 6
- mlip_forces: bfloat16 [18432, 1024], P(('col', 'cfg'), 'row'), may hold values from -6 to 6
- frequency: float32 [18432], P(('col', 'cfg')), may hold values from 0.25 to 4
Outputs:
- gradient: float32 [18432, 18432], P(('col', 'cfg'), 'row')
The draws below stay inside these ranges and needn't reach their ends.
All inputs are finite; a program needn't handle non-finite values.
Results may differ from the reference program's by a relative error of at most 0.0055.
Values may be sent and summed in bfloat16 or wider, within the bound.
A program may use at most 64 MiB of HBM per device.

```python
import math
import jax
import jax.numpy as jnp

NMODES = 18432
CONFIGS = 1024


def strengthened(values, own_key, source, target, parts, factor):
    owner, partner = [(jnp.arange(values.shape[position]) // (values.shape[position] // parts)).reshape([-1 if axis == position else 1 for axis in range(values.ndim)]) for position in (source, target)]
    chosen = jax.random.permutation(own_key, parts)[partner]
    strong = (owner == chosen) | (owner == (partner + parts // 2) % parts)
    return jnp.where(strong, factor * values, values)


def levels(stream_key, shape, shards, low, top_value):
    factor_of = 1.0
    for dim, shards_of in shards:
        steps = jax.random.uniform(jax.random.fold_in(jax.random.fold_in(stream_key, 6), dim), (shards_of,), jnp.float32, low / len(shards), top_value / len(shards))
        factor_of = factor_of * jnp.repeat(jnp.exp(steps), shape[dim] // shards_of).reshape((-1,) + (1,) * (len(shape) - 1 - dim))
    return factor_of


def bell_draw(rng, dims, width, reach, shards=(), kind=jnp.bfloat16):
    entries = width * jax.random.normal(rng, dims, jnp.float32)
    if shards:
        entries = entries * levels(rng, dims, shards, -0.22, 0.18)
    return jnp.clip(entries, -reach, reach).astype(kind)


def noise_with(stream_key, extent, spread, bound, pieces, heavy, kind=jnp.bfloat16):
    result = spread * jax.random.normal(stream_key, extent, jnp.float32)
    if pieces:
        result = result * levels(stream_key, extent, pieces, -0.22, 0.18)
    return jnp.clip(strengthened(result, jax.random.fold_in(stream_key, 3), *heavy), -bound, bound).astype(kind)


def setup_inputs(seed: int = 0) -> dict:
    splits = jax.random.split(jax.random.key(seed), 6)
    eigvec = bell_draw(splits[0], (NMODES, NMODES), NMODES ** -0.5, 0.046875, ((0, 8), (1, 32)))
    force_const = bell_draw(splits[1], (NMODES, NMODES), NMODES ** -0.5, 0.046875, ((0, 32), (1, 8)))
    amplitudes = noise_with(splits[2], (NMODES, CONFIGS), 1.0, 6.0, ((0, 32),), (0, 1, 32, 2.75))
    mlip_forces = bell_draw(splits[3], (NMODES, CONFIGS), 1.0, 6.0, ((0, 32), (1, 8)))
    frequency = jnp.clip(jnp.exp(math.log(4.0) - 2.7725887 * jax.random.uniform(splits[4], (NMODES,), jnp.float32) ** levels(splits[4], (NMODES,), ((0, 32),), -0.2, 0.2)), 0.25, 4.0)
    return {"eigvec": eigvec, "force_const": force_const, "amplitudes": amplitudes, "mlip_forces": mlip_forces, "frequency": frequency}


def reference(eigvec, force_const, amplitudes, mlip_forces, frequency):
    mode_scale = 1.0 / jnp.sqrt(2.0 * frequency)
    scaled_amp = (mode_scale[:, None] * amplitudes.astype(jnp.float32)).astype(jnp.bfloat16)
    displaced = jnp.dot(eigvec, scaled_amp, preferred_element_type=jnp.float32).astype(jnp.bfloat16)
    harmonic = jnp.dot(force_const, displaced, preferred_element_type=jnp.float32)
    residual = (mlip_forces.astype(jnp.float32) + harmonic).astype(jnp.bfloat16)
    total = jnp.dot(residual, displaced.T, preferred_element_type=jnp.float32)
    return total / jnp.sqrt(jnp.float32(CONFIGS))
```

```python
import functools

import jax
import jax.numpy as jnp
from jax import lax
from jax.experimental import pallas as pl
from jax.experimental.pallas import tpu as pltpu
from jax.sharding import PartitionSpec as P

MESH = pl.DeviceIdType.MESH
PAIRS = 4
LANES = 128
ORDER = [(8, 2), (4, 1), (0, 0), (9, 2), (5, 1), (1, 0), (10, 2), (6, 1), (2, 0), (11, 2), (7, 1), (3, 0)]


def comm_kernel(
    eig_hbm, fc_hbm, amp_hbm, forces_hbm, freq_ref, resid_hbm, disp_hbm,
    eig, fc, amp, scale, part32, part16, in_opp, in_near, sum32, sum16, in_second, own32, own16, in_zl,
    disp, harm, in_core, harm32, harm16, in_zh, force_in, force_own, resid,
    load_sem, col_send, col_recv, row_send, row_recv, m_send, m_recv, out_sem,
):
    rows = eig_hbm.shape[0]
    quarter, sub = rows // 4, rows // 16
    half = quarter // 2
    out_rows = fc_hbm.shape[0]
    piece = out_rows // 4

    row, x, cfg = lax.axis_index("row"), lax.axis_index("col"), lax.axis_index("cfg")
    zh, core, y, zl = row // 2, row % 2, cfg // 2, cfg % 2

    def x_dev(d):
        return {"col": (x + d) % 4}

    def y_dev(d):
        return {"cfg": ((y + d) % 4) * 2 + zl}

    def zh_dev(d):
        return {"row": ((zh + d) % 4) * 2 + core}

    zl_dev = {"cfg": y * 2 + (1 - zl)}
    core_dev = {"row": zh * 2 + (1 - core)}
    axes = [(x, x_dev, y, y_dev), (y, y_dev, x, x_dev)]

    loads = [pltpu.make_async_copy(amp_hbm.at[:, pl.ds(p * 2 * LANES, 2 * LANES)], amp.at[p], load_sem.at[p]) for p in range(PAIRS)]
    loads += [pltpu.make_async_copy(eig_hbm.at[pl.ds(q * quarter, quarter)], eig.at[q], load_sem.at[4 + q]) for q in range(4)]
    load_fc = pltpu.make_async_copy(fc_hbm, fc, load_sem.at[8])
    load_forces = [pltpu.make_async_copy(forces_hbm.at[pl.ds(q * piece, piece)], force_own.at[q], load_sem.at[9 + q]) for q in range(4)]
    for c in loads:
        c.start()
    for c in load_forces:
        c.start()
    load_fc.start()

    barrier = pltpu.get_barrier_semaphore()
    peers = [x_dev(1), x_dev(2), x_dev(3), y_dev(1), y_dev(2), y_dev(3), zh_dev(1), zh_dev(2), zh_dev(3), zl_dev, core_dev]
    for dev in peers:
        pl.semaphore_signal(barrier, inc=1, device_id=dev, device_id_type=MESH)

    modes = scale.shape[0]
    f = freq_ref[...].reshape(1, modes)
    on_diag = lax.broadcasted_iota(jnp.int32, (modes, modes), 0) == lax.broadcasted_iota(jnp.int32, (modes, modes), 1)
    f_col = jnp.sum(jnp.where(on_diag, f, 0.0), axis=1, keepdims=True)
    scale[...] = jnp.broadcast_to(1.0 / jnp.sqrt(2.0 * f_col), scale.shape)

    for c in loads:
        c.wait()
    for c in load_forces:
        c.wait()

    def col_copy(p, t, k, src, dst, dev):
        return pltpu.make_async_remote_copy(
            src_ref=src, dst_ref=dst, send_sem=col_send.at[p, t, k], recv_sem=col_recv.at[p, t, k],
            device_id=dev, device_id_type=MESH,
        )

    def row_copy(p, k, src, dst, dev):
        return pltpu.make_async_remote_copy(
            src_ref=src, dst_ref=dst, send_sem=row_send.at[p, k], recv_sem=row_recv.at[p, k],
            device_id=dev, device_id_type=MESH,
        )

    lo, hi = pl.ds(0, half), pl.ds(half, half)

    def first_out(p, t, k):
        a, a_dev, _, _ = axes[t]
        q1, q2, q3 = (a + 1) % 4, (a + 2) % 4, (a + 3) % 4
        src, dst, dev = [
            (part16.at[p, t, q2, lo], in_opp.at[p, t, 0], 1),
            (part16.at[p, t, q2, hi], in_opp.at[p, t, 1], 3),
            (part16.at[p, t, q1, hi], in_near.at[p, t, 0, hi], 1),
            (part16.at[p, t, q3, lo], in_near.at[p, t, 1, lo], 3),
            (part16.at[p, t, q1, lo], in_near.at[p, t, 0, lo], 1),
            (part16.at[p, t, q3, hi], in_near.at[p, t, 1, hi], 3),
        ][k]
        return col_copy(p, t, k, src, dst, a_dev(dev))

    def second_out(p, t, d):
        _, _, b, b_dev = axes[t]
        return col_copy(p, t, 5 + d, sum16.at[p, t, (b + d) % 4], in_second.at[p, t, d - 1], b_dev(d))

    def zl_out(p, t):
        return col_copy(p, t, 9, own16.at[p, t], in_zl.at[p, t], zl_dev)

    def disp_at(p, t, start, size, align):
        return disp.at[p, pl.ds(pl.multiple_of(start, align), size), pl.ds(t * LANES, LANES)]

    def spread_b(p, t, d, owner):
        a, _, _, b_dev = axes[t]
        at = disp_at(p, t, a * quarter + owner * sub, sub, 16)
        return col_copy(p, t, 9 + d, at, at, b_dev(d))

    def spread_a(p, t, k, owner):
        _, a_dev, _, _ = axes[t]
        which, dev = [(0, 1), (1, 1), (1, 3), (0, 3), (0, 1), (1, 3)][k]
        at = disp_at(p, t, owner * quarter + which * half, half, 16)
        return col_copy(p, t, 13 + k, at, at, a_dev(dev))

    def core_out(p):
        return row_copy(p, 0, harm.at[p, 1 - core], in_core.at[p], core_dev)

    def zh_out(p, d):
        return row_copy(p, d, harm16.at[p, (zh + d) % 4], in_zh.at[p, d - 1], zh_dev(d))

    def resid_spread(p, d, owner):
        at = resid.at[p, core, owner]
        return row_copy(p, 3 + d, at, at, zh_dev(d))

    def resid_core(p, which):
        at = resid.at[p, which]
        return row_copy(p, 7, at, at, core_dev)

    def force_out(d, slot):
        return pltpu.make_async_remote_copy(
            src_ref=force_own.at[(zh + d) % 4], dst_ref=force_in.at[slot],
            send_sem=m_send.at[d - 1], recv_sem=m_recv.at[d - 1], device_id=zh_dev(d), device_id_type=MESH,
        )

    def compute_part(p):
        scaled = (scale[:, :1] * amp[p].astype(jnp.float32)).astype(jnp.bfloat16)

        def one(q, carry):
            product = jnp.dot(eig[q], scaled, preferred_element_type=jnp.float32)
            for t in range(2):
                block = product[:, t * LANES : (t + 1) * LANES]
                part32[p, t, q] = block
                part16[p, t, q] = block.astype(jnp.bfloat16)
            return carry

        lax.fori_loop(0, 4, one, 0)

    def send_part(p):
        for k in range(4):
            for t in range(2):
                first_out(p, t, k).start()

    def stage0(p):
        @pl.when(p > 0)
        def _():
            compute_part(p)
            send_part(p)

    def stage1(p):
        for t in range(2):
            a = axes[t][0]
            first_out(p, t, 0).wait_recv()
            q1, q3 = (a + 1) % 4, (a + 3) % 4
            part16[p, t, q1, lo] = (part32[p, t, q1, lo] + in_opp[p, t, 0].astype(jnp.float32)).astype(jnp.bfloat16)
            first_out(p, t, 4).start()
            first_out(p, t, 1).wait_recv()
            part16[p, t, q3, hi] = (part32[p, t, q3, hi] + in_opp[p, t, 1].astype(jnp.float32)).astype(jnp.bfloat16)
            first_out(p, t, 5).start()

    def stage2(p):
        for t in range(2):
            a, _, b, _ = axes[t]
            for k in range(2, 6):
                first_out(p, t, k).wait_recv()
            total = part32[p, t, a] + in_near[p, t, 0].astype(jnp.float32) + in_near[p, t, 1].astype(jnp.float32)
            total = total.reshape(4, sub, LANES)
            sum32[p, t] = total
            sum16[p, t] = total.astype(jnp.bfloat16)
            for d in (2, 1, 3):
                second_out(p, t, d).start()

    def stage3(p):
        for t in range(2):
            b = axes[t][2]
            for d in (1, 2, 3):
                second_out(p, t, d).wait_recv()
            total = sum32[p, t, b]
            for d in range(3):
                total += in_second[p, t, d].astype(jnp.float32)
            own32[p, t] = total
            own16[p, t] = total.astype(jnp.bfloat16)
            zl_out(p, t).start()

    def stage4(p):
        for t in range(2):
            a, _, b, _ = axes[t]
            zl_out(p, t).wait_recv()
            value = (own32[p, t] + in_zl[p, t].astype(jnp.float32)).astype(jnp.bfloat16)
            disp[p, pl.ds(pl.multiple_of(a * quarter + b * sub, 16), sub), pl.ds(t * LANES, LANES)] = value
            for d in (2, 1, 3):
                spread_b(p, t, d, b).start()

    def stage5(p):
        for t in range(2):
            a, _, b, _ = axes[t]
            for d in (1, 2, 3):
                spread_b(p, t, d, (b + 4 - d) % 4).wait_recv()
            for k in (0, 2, 1, 3):
                spread_a(p, t, k, a).start()

    def stage6(p):
        for t in range(2):
            a = axes[t][0]
            below, above = (a + 3) % 4, (a + 1) % 4
            spread_a(p, t, 0, below).wait_recv()
            spread_a(p, t, 4, below).start()
            spread_a(p, t, 2, above).wait_recv()
            spread_a(p, t, 5, above).start()

    def stage7(p):
        for t in range(2):
            a = axes[t][0]
            below, above, far = (a + 3) % 4, (a + 1) % 4, (a + 2) % 4
            spread_a(p, t, 1, below).wait_recv()
            spread_a(p, t, 3, above).wait_recv()
            spread_a(p, t, 4, far).wait_recv()
            spread_a(p, t, 5, far).wait_recv()
        pltpu.make_async_copy(disp.at[p], disp_hbm.at[p], out_sem.at[p, 0]).start()

        @pl.when(p == 0)
        def _():
            load_fc.wait()
            for d in (1, 2, 3):
                force_out(d, (zh + 4 - d) % 4).wait_recv()

        product = jnp.dot(fc[...], disp[p], preferred_element_type=jnp.float32)
        for t in range(2):
            harm[p, t] = product[:, t * LANES : (t + 1) * LANES]
        core_out(p).start()

    def stage8(p):
        core_out(p).wait_recv()
        total = (harm[p, core] + in_core[p]).reshape(4, piece, LANES)
        harm32[p] = total
        harm16[p] = total.astype(jnp.bfloat16)
        for d in (2, 1, 3):
            zh_out(p, d).start()

    def stage9(p):
        for d in (1, 2, 3):
            zh_out(p, d).wait_recv()
        total = force_in[p].astype(jnp.float32) + harm32[p, zh]
        for d in range(3):
            total += in_zh[p, d].astype(jnp.float32)
        resid[p, core, zh] = total.astype(jnp.bfloat16)
        for d in (2, 1, 3):
            resid_spread(p, d, zh).start()

    def stage10(p):
        for d in (1, 2, 3):
            resid_spread(p, d, (zh + 4 - d) % 4).wait_recv()
        resid_core(p, core).start()

    def stage11(p):
        resid_core(p, 1 - core).wait_recv()
        pltpu.make_async_copy(resid.at[p], resid_hbm.at[p], out_sem.at[p, 1]).start()

    stages = [stage0, stage1, stage2, stage3, stage4, stage5, stage6, stage7, stage8, stage9, stage10, stage11]

    compute_part(0)
    force_in[zh] = force_own[zh]
    pl.semaphore_wait(barrier, len(peers))
    send_part(0)
    for d in (1, 2, 3):
        force_out(d, zh).start()

    def turn(u, carry):
        for s, offset in ORDER:
            p = u - offset

            @pl.when((p >= 0) & (p < PAIRS))
            def _(s=s, p=p):
                stages[s](p)

        return carry

    lax.fori_loop(0, PAIRS + max(o for _, o in ORDER), turn, 0)

    def drain(p, carry):
        for t in range(2):
            a, _, b, _ = axes[t]
            for k in range(6):
                first_out(p, t, k).wait_send()
                spread_a(p, t, k, a).wait_send()
            for d in (1, 2, 3):
                second_out(p, t, d).wait_send()
                spread_b(p, t, d, b).wait_send()
            zl_out(p, t).wait_send()
        core_out(p).wait_send()
        for d in (1, 2, 3):
            zh_out(p, d).wait_send()
            resid_spread(p, d, zh).wait_send()
        resid_core(p, core).wait_send()
        pltpu.make_async_copy(disp.at[p], disp_hbm.at[p], out_sem.at[p, 0]).wait()
        pltpu.make_async_copy(resid.at[p], resid_hbm.at[p], out_sem.at[p, 1]).wait()
        return carry

    lax.fori_loop(0, PAIRS, drain, 0)
    for d in (1, 2, 3):
        force_out(d, zh).wait_send()


def exchange(eigvec, force_const, amplitudes, mlip_forces, frequency):
    rows, modes = eigvec.shape
    out_rows = force_const.shape[0]
    quarter, sub, piece = rows // 4, rows // 16, out_rows // 4
    half = quarter // 2
    bf16, f32 = jnp.bfloat16, jnp.float32
    anywhere = pl.BlockSpec(memory_space=pl.ANY)
    dma = pltpu.SemaphoreType.DMA
    return pl.pallas_call(
        comm_kernel,
        name="exchange",
        out_shape=[
            jax.ShapeDtypeStruct((PAIRS, 2, 4, piece, LANES), bf16),
            jax.ShapeDtypeStruct((PAIRS, rows, 2 * LANES), bf16),
        ],
        in_specs=[anywhere] * 4 + [pl.BlockSpec(memory_space=pltpu.VMEM)],
        out_specs=[anywhere, anywhere],
        scratch_shapes=[
            pltpu.VMEM((4, quarter, modes), bf16),
            pltpu.VMEM((out_rows, rows), bf16),
            pltpu.VMEM((PAIRS, modes, 2 * LANES), bf16),
            pltpu.VMEM((modes, LANES), f32),
            pltpu.VMEM((PAIRS, 2, 4, quarter, LANES), f32),
            pltpu.VMEM((PAIRS, 2, 4, quarter, LANES), bf16),
            pltpu.VMEM((PAIRS, 2, 2, half, LANES), bf16),
            pltpu.VMEM((PAIRS, 2, 2, quarter, LANES), bf16),
            pltpu.VMEM((PAIRS, 2, 4, sub, LANES), f32),
            pltpu.VMEM((PAIRS, 2, 4, sub, LANES), bf16),
            pltpu.VMEM((PAIRS, 2, 3, sub, LANES), bf16),
            pltpu.VMEM((PAIRS, 2, sub, LANES), f32),
            pltpu.VMEM((PAIRS, 2, sub, LANES), bf16),
            pltpu.VMEM((PAIRS, 2, sub, LANES), bf16),
            pltpu.VMEM((PAIRS, rows, 2 * LANES), bf16),
            pltpu.VMEM((PAIRS, 2, out_rows, LANES), f32),
            pltpu.VMEM((PAIRS, out_rows, LANES), f32),
            pltpu.VMEM((PAIRS, 4, piece, LANES), f32),
            pltpu.VMEM((PAIRS, 4, piece, LANES), bf16),
            pltpu.VMEM((PAIRS, 3, piece, LANES), bf16),
            pltpu.VMEM((PAIRS, piece, LANES), bf16),
            pltpu.VMEM((4, piece, LANES), bf16),
            pltpu.VMEM((PAIRS, 2, 4, piece, LANES), bf16),
            dma((13,)),
            dma((PAIRS, 2, 19)),
            dma((PAIRS, 2, 19)),
            dma((PAIRS, 8)),
            dma((PAIRS, 8)),
            dma((3,)),
            dma((3,)),
            dma((PAIRS, 2)),
        ],
        compiler_params=pltpu.CompilerParams(
            collective_id=0, has_side_effects=True, vmem_limit_bytes=60 << 20
        ),
    )(eigvec, force_const, amplitudes, mlip_forces, frequency)


def local(eigvec, force_const, amplitudes, mlip_forces, frequency):
    resid, disp = exchange(eigvec, force_const, amplitudes, mlip_forces, frequency)
    out_rows = force_const.shape[0]
    resid = resid.transpose(2, 3, 0, 1, 4).reshape(out_rows, -1)
    disp = disp.transpose(1, 0, 2).reshape(disp.shape[1], -1)
    total = lax.dot_general(resid, disp, (((1,), (1,)), ((), ())), preferred_element_type=jnp.float32)
    return total * (1.0 / 32.0)


def solution(mesh):
    return jax.shard_map(
        local,
        mesh=mesh,
        in_specs=(
            P("row", ("col", "cfg")),
            P(("col", "cfg"), "row"),
            P(("col", "cfg"), None),
            P(("col", "cfg"), "row"),
            P(("col", "cfg")),
        ),
        out_specs=P(("col", "cfg"), "row"),
        check_vma=False,
    )
```

```python
import functools

import jax
import jax.numpy as jnp
from jax import lax
from jax.experimental import pallas as pl
from jax.experimental.pallas import tpu as pltpu
from jax.sharding import PartitionSpec as P

MESH = pl.DeviceIdType.MESH
PAIRS = 4
LANES = 128
TILE = 256
ORDER = [
    (0, 0), (1, 0, 0), (1, 0, 1), (0, 1), (2, 0, 0), (2, 0, 1), (1, 1, 0), (1, 1, 1),
    (0, 2), (0, 3), (3, 0, 0), (3, 0, 1), (2, 1, 0), (2, 1, 1), (1, 2, 0), (1, 2, 1),
    (4, 0, 0), (4, 0, 1), (1, 3, 0), (1, 3, 1), (3, 1, 0), (3, 1, 1), (2, 2, 0), (2, 2, 1),
    (5, 0, 0), (5, 0, 1), (4, 1, 0), (4, 1, 1), (2, 3, 0), (2, 3, 1), (3, 2, 0), (3, 2, 1),
    (6, 0, 1), (6, 0, 0), (4, 2, 0), (4, 2, 1), (5, 1, 0), (5, 1, 1), (3, 3, 0), (3, 3, 1),
    (7, 0), (5, 2, 0), (5, 2, 1), (4, 3, 0), (4, 3, 1), (8, 0), (6, 1, 1), (6, 1, 0),
    (6, 2, 1), (6, 2, 0), (5, 3, 0), (5, 3, 1), (9, 0), (7, 1), (7, 2), (8, 1),
    (6, 3, 1), (6, 3, 0), (8, 2), (7, 3), (10, 0), (8, 3), (11, 0), (12, 0, 0),
    (9, 1), (12, 0, 1), (12, 0, 2), (9, 2), (9, 3), (10, 1), (11, 1), (12, 1, 0),
    (12, 1, 1), (12, 1, 2), (10, 2), (11, 2), (12, 2, 0), (12, 2, 1), (10, 3), (12, 2, 2),
    (11, 3),
]


def comm_kernel(
    eig_hbm, fc_hbm, amp_hbm, forces_hbm, freq_ref, grad_hbm, resid_hbm, disp_hbm,
    eig_t, eig, fc, amp, scale, part32, part16, in_opp, in_near, sum32, sum16, in_second, own32, own16, in_zl,
    disp, harm, in_core, harm32, harm16, in_zh, force_in, force_own, resid, grad,
    load_sem, col_send, col_recv, row_send, row_recv, m_send, m_recv, out_sem,
):
    modes, rows = eig_hbm.shape
    quarter, sub = rows // 4, rows // 16
    half = quarter // 2
    out_rows = fc_hbm.shape[0]
    piece = out_rows // 4

    row, x, cfg = lax.axis_index("row"), lax.axis_index("col"), lax.axis_index("cfg")
    zh, core, y, zl = row // 2, row % 2, cfg // 2, cfg % 2

    def x_dev(d):
        return {"col": (x + d) % 4}

    def y_dev(d):
        return {"cfg": ((y + d) % 4) * 2 + zl}

    def zh_dev(d):
        return {"row": ((zh + d) % 4) * 2 + core}

    zl_dev = {"cfg": y * 2 + (1 - zl)}
    core_dev = {"row": zh * 2 + (1 - core)}
    axes = [(x, x_dev, y, y_dev), (y, y_dev, x, x_dev)]

    loads = [pltpu.make_async_copy(amp_hbm.at[:, pl.ds(p * 2 * LANES, 2 * LANES)], amp.at[p], load_sem.at[p]) for p in range(PAIRS)]
    loads += [pltpu.make_async_copy(eig_hbm.at[:, pl.ds(q * TILE, TILE)], eig_t.at[q], load_sem.at[13 + q]) for q in range(rows // TILE)]
    load_fc = pltpu.make_async_copy(fc_hbm, fc, load_sem.at[8])
    load_forces = [pltpu.make_async_copy(forces_hbm.at[pl.ds(q * piece, piece)], force_own.at[q], load_sem.at[9 + q]) for q in range(4)]
    for c in loads:
        c.start()
    for c in load_forces:
        c.start()
    load_fc.start()

    barrier = pltpu.get_barrier_semaphore()
    peers = [x_dev(1), x_dev(2), x_dev(3), y_dev(1), y_dev(2), y_dev(3), zh_dev(1), zh_dev(2), zh_dev(3), zl_dev, core_dev]
    for dev in peers:
        pl.semaphore_signal(barrier, inc=1, device_id=dev, device_id_type=MESH)

    f = freq_ref[...].reshape(1, modes)
    on_diag = lax.broadcasted_iota(jnp.int32, (modes, modes), 0) == lax.broadcasted_iota(jnp.int32, (modes, modes), 1)
    f_col = jnp.sum(jnp.where(on_diag, f, 0.0), axis=1, keepdims=True)
    scale[...] = jnp.broadcast_to(1.0 / jnp.sqrt(2.0 * f_col), scale.shape)

    for c in loads:
        c.wait()
    for c in load_forces:
        c.wait()

    def flip(q, carry):
        eig[pl.ds(pl.multiple_of(q * TILE, TILE), TILE)] = eig_t[q].T
        return carry

    lax.fori_loop(0, rows // TILE, flip, 0)

    def col_copy(p, t, k, src, dst, dev):
        return pltpu.make_async_remote_copy(
            src_ref=src, dst_ref=dst, send_sem=col_send.at[p, t, k], recv_sem=col_recv.at[p, t, k],
            device_id=dev, device_id_type=MESH,
        )

    def row_copy(p, k, src, dst, dev):
        return pltpu.make_async_remote_copy(
            src_ref=src, dst_ref=dst, send_sem=row_send.at[p, k], recv_sem=row_recv.at[p, k],
            device_id=dev, device_id_type=MESH,
        )

    lo, hi = pl.ds(0, half), pl.ds(half, half)

    def first_out(p, t, k):
        a, a_dev, _, _ = axes[t]
        q1, q2, q3 = (a + 1) % 4, (a + 2) % 4, (a + 3) % 4
        src, dst, dev = [
            (part16.at[p, t, q2, lo], in_opp.at[p, t, 0], 1),
            (part16.at[p, t, q2, hi], in_opp.at[p, t, 1], 3),
            (part16.at[p, t, q1, hi], in_near.at[p, t, 0, hi], 1),
            (part16.at[p, t, q3, lo], in_near.at[p, t, 1, lo], 3),
            (part16.at[p, t, q1, lo], in_near.at[p, t, 0, lo], 1),
            (part16.at[p, t, q3, hi], in_near.at[p, t, 1, hi], 3),
        ][k]
        return col_copy(p, t, k, src, dst, a_dev(dev))

    def second_out(p, t, d):
        _, _, b, b_dev = axes[t]
        return col_copy(p, t, 5 + d, sum16.at[p, t, (b + d) % 4], in_second.at[p, t, d - 1], b_dev(d))

    def zl_out(p, t):
        return col_copy(p, t, 9, own16.at[p, t], in_zl.at[p, t], zl_dev)

    def disp_at(p, t, start, size, align):
        return disp.at[p, t, pl.ds(pl.multiple_of(start, align), size)]

    def spread_b(p, t, d, owner):
        a, _, _, b_dev = axes[t]
        at = disp_at(p, t, a * quarter + owner * sub, sub, 16)
        return col_copy(p, t, 9 + d, at, at, b_dev(d))

    def spread_a(p, t, k, owner):
        _, a_dev, _, _ = axes[t]
        which, dev = [(0, 1), (1, 1), (1, 3), (0, 3), (0, 1), (1, 3)][k]
        at = disp_at(p, t, owner * quarter + which * half, half, 16)
        return col_copy(p, t, 13 + k, at, at, a_dev(dev))

    def core_out(p):
        return row_copy(p, 0, harm.at[p, 1 - core], in_core.at[p], core_dev)

    def zh_out(p, d):
        return row_copy(p, d, harm16.at[p, (zh + d) % 4], in_zh.at[p, d - 1], zh_dev(d))

    def resid_spread(p, d, owner):
        at = resid.at[p, core, pl.ds(pl.multiple_of(owner * piece, 16), piece)]
        return row_copy(p, 3 + d, at, at, zh_dev(d))

    def resid_core(p, which):
        at = resid.at[p, which]
        return row_copy(p, 7, at, at, core_dev)

    def disp_store(t):
        return pltpu.make_async_copy(disp.at[PAIRS - 1, t], disp_hbm.at[:, pl.ds(t * LANES, LANES)], out_sem.at[t])

    def resid_store(t):
        return pltpu.make_async_copy(resid.at[PAIRS - 1, t], resid_hbm.at[:, pl.ds(t * LANES, LANES)], out_sem.at[2 + t])

    def grad_store(g):
        at = pl.ds(g * 3 * TILE, 3 * TILE)
        return pltpu.make_async_copy(grad.at[:, at], grad_hbm.at[:, at], out_sem.at[4 + g])

    def force_out(d, slot):
        return pltpu.make_async_remote_copy(
            src_ref=force_own.at[(zh + d) % 4], dst_ref=force_in.at[slot],
            send_sem=m_send.at[d - 1], recv_sem=m_recv.at[d - 1], device_id=zh_dev(d), device_id_type=MESH,
        )

    def compute_part(p):
        scaled = (scale[:, :1] * amp[p].astype(jnp.float32)).astype(jnp.bfloat16)

        def one(q, carry):
            product = jnp.dot(eig[pl.ds(pl.multiple_of(q * quarter, 16), quarter)], scaled, preferred_element_type=jnp.float32)
            for t in range(2):
                block = product[:, t * LANES : (t + 1) * LANES]
                part32[p, t, q] = block
                part16[p, t, q] = block.astype(jnp.bfloat16)
            return carry

        lax.fori_loop(0, 4, one, 0)

    def send_part(p):
        for k in range(4):
            for t in range(2):
                first_out(p, t, k).start()

    def stage0(p):
        compute_part(p)
        if p == 0:
            pl.semaphore_wait(barrier, len(peers))
        send_part(p)
        if p == 0:
            for d in (1, 2, 3):
                force_out(d, zh).start()

    def stage1(p, t):
        a = axes[t][0]
        first_out(p, t, 0).wait_recv()
        q1, q3 = (a + 1) % 4, (a + 3) % 4
        part16[p, t, q1, lo] = (part32[p, t, q1, lo] + in_opp[p, t, 0].astype(jnp.float32)).astype(jnp.bfloat16)
        first_out(p, t, 4).start()
        first_out(p, t, 1).wait_recv()
        part16[p, t, q3, hi] = (part32[p, t, q3, hi] + in_opp[p, t, 1].astype(jnp.float32)).astype(jnp.bfloat16)
        first_out(p, t, 5).start()

    def stage2(p, t):
        a, _, b, _ = axes[t]
        for k in range(2, 6):
            first_out(p, t, k).wait_recv()
        total = part32[p, t, a] + in_near[p, t, 0].astype(jnp.float32) + in_near[p, t, 1].astype(jnp.float32)
        total = total.reshape(4, sub, LANES)
        sum32[p, t] = total
        sum16[p, t] = total.astype(jnp.bfloat16)
        for d in (2, 1, 3):
            second_out(p, t, d).start()

    def stage3(p, t):
        b = axes[t][2]
        for d in (1, 2, 3):
            second_out(p, t, d).wait_recv()
        total = sum32[p, t, b]
        for d in range(3):
            total += in_second[p, t, d].astype(jnp.float32)
        own32[p, t] = total
        own16[p, t] = total.astype(jnp.bfloat16)
        zl_out(p, t).start()

    def stage4(p, t):
        a, _, b, _ = axes[t]
        zl_out(p, t).wait_recv()
        value = (own32[p, t] + in_zl[p, t].astype(jnp.float32)).astype(jnp.bfloat16)
        disp[p, t, pl.ds(pl.multiple_of(a * quarter + b * sub, 16), sub)] = value
        for d in (2, 1, 3):
            spread_b(p, t, d, b).start()

    def stage5(p, t):
        a, _, b, _ = axes[t]
        for d in (1, 2, 3):
            spread_b(p, t, d, (b + 4 - d) % 4).wait_recv()
        for k in (0, 2, 1, 3):
            spread_a(p, t, k, a).start()

    def stage6(p, t):
        a = axes[t][0]
        below, above = (a + 3) % 4, (a + 1) % 4
        spread_a(p, t, 0, below).wait_recv()
        spread_a(p, t, 4, below).start()
        spread_a(p, t, 2, above).wait_recv()
        spread_a(p, t, 5, above).start()

    def stage7(p):
        for t in range(2):
            a = axes[t][0]
            below, above, far = (a + 3) % 4, (a + 1) % 4, (a + 2) % 4
            spread_a(p, t, 1, below).wait_recv()
            spread_a(p, t, 3, above).wait_recv()
            spread_a(p, t, 4, far).wait_recv()
            spread_a(p, t, 5, far).wait_recv()
        if p == PAIRS - 1:
            for t in range(2):
                disp_store(t).start()
        if p == 0:
            load_fc.wait()
            for d in (1, 2, 3):
                force_out(d, (zh + 4 - d) % 4).wait_recv()

        product = jnp.dot(fc[...], jnp.concatenate([disp[p, 0], disp[p, 1]], axis=1), preferred_element_type=jnp.float32)
        for t in range(2):
            harm[p, t] = product[:, t * LANES : (t + 1) * LANES]
        core_out(p).start()

    def stage8(p):
        core_out(p).wait_recv()
        total = (harm[p, core] + in_core[p]).reshape(4, piece, LANES)
        harm32[p] = total
        harm16[p] = total.astype(jnp.bfloat16)
        for d in (2, 1, 3):
            zh_out(p, d).start()

    def stage9(p):
        for d in (1, 2, 3):
            zh_out(p, d).wait_recv()
        total = force_in[p].astype(jnp.float32) + harm32[p, zh]
        for d in range(3):
            total += in_zh[p, d].astype(jnp.float32)
        resid[p, core, pl.ds(pl.multiple_of(zh * piece, 16), piece)] = total.astype(jnp.bfloat16)
        for d in (2, 1, 3):
            resid_spread(p, d, zh).start()

    def stage10(p):
        for d in (1, 2, 3):
            resid_spread(p, d, (zh + 4 - d) % 4).wait_recv()
        resid_core(p, core).start()

    def stage11(p):
        resid_core(p, 1 - core).wait_recv()
        if p == PAIRS - 1:
            for t in range(2):
                resid_store(t).start()

    def stage12(p, g):
        left = jnp.concatenate([resid[p, 0], resid[p, 1]], axis=1)
        for c in range(g * 3, g * 3 + 3):
            at = pl.ds(c * TILE, TILE)
            right = jnp.concatenate([disp[p, 0, at], disp[p, 1, at]], axis=1)
            term = lax.dot_general(left, right, (((1,), (1,)), ((), ())), preferred_element_type=jnp.float32)
            if p > 0:
                term += grad[:, at]
            grad[:, at] = term
        if p == PAIRS - 2:
            grad_store(g).start()

    stages = [stage0, stage1, stage2, stage3, stage4, stage5, stage6, stage7, stage8, stage9, stage10, stage11, stage12]
    force_in[zh] = force_own[zh]
    for s, *which in ORDER:
        stages[s](*which)

    def drain(p, carry):
        for t in range(2):
            a, _, b, _ = axes[t]
            for k in range(6):
                first_out(p, t, k).wait_send()
                spread_a(p, t, k, a).wait_send()
            for d in (1, 2, 3):
                second_out(p, t, d).wait_send()
                spread_b(p, t, d, b).wait_send()
            zl_out(p, t).wait_send()
        core_out(p).wait_send()
        for d in (1, 2, 3):
            zh_out(p, d).wait_send()
            resid_spread(p, d, zh).wait_send()
        resid_core(p, core).wait_send()
        return carry

    lax.fori_loop(0, PAIRS, drain, 0)
    for t in range(2):
        disp_store(t).wait()
        resid_store(t).wait()
    for g in range(3):
        grad_store(g).wait()
    for d in (1, 2, 3):
        force_out(d, zh).wait_send()


def exchange(eigvec, force_const, amplitudes, mlip_forces, frequency):
    modes, rows = eigvec.shape
    out_rows = force_const.shape[0]
    quarter, sub, piece = rows // 4, rows // 16, out_rows // 4
    half = quarter // 2
    bf16, f32 = jnp.bfloat16, jnp.float32
    anywhere = pl.BlockSpec(memory_space=pl.ANY)
    dma = pltpu.SemaphoreType.DMA
    return pl.pallas_call(
        comm_kernel,
        name="exchange",
        out_shape=[
            jax.ShapeDtypeStruct((out_rows, rows), f32),
            jax.ShapeDtypeStruct((out_rows, 2 * LANES), bf16),
            jax.ShapeDtypeStruct((rows, 2 * LANES), bf16),
        ],
        in_specs=[anywhere] * 4 + [pl.BlockSpec(memory_space=pltpu.VMEM)],
        out_specs=[anywhere] * 3,
        scratch_shapes=[
            pltpu.VMEM((rows // TILE, modes, TILE), bf16),
            pltpu.VMEM((rows, modes), bf16),
            pltpu.VMEM((out_rows, rows), bf16),
            pltpu.VMEM((PAIRS, modes, 2 * LANES), bf16),
            pltpu.VMEM((modes, LANES), f32),
            pltpu.VMEM((PAIRS, 2, 4, quarter, LANES), f32),
            pltpu.VMEM((PAIRS, 2, 4, quarter, LANES), bf16),
            pltpu.VMEM((PAIRS, 2, 2, half, LANES), bf16),
            pltpu.VMEM((PAIRS, 2, 2, quarter, LANES), bf16),
            pltpu.VMEM((PAIRS, 2, 4, sub, LANES), f32),
            pltpu.VMEM((PAIRS, 2, 4, sub, LANES), bf16),
            pltpu.VMEM((PAIRS, 2, 3, sub, LANES), bf16),
            pltpu.VMEM((PAIRS, 2, sub, LANES), f32),
            pltpu.VMEM((PAIRS, 2, sub, LANES), bf16),
            pltpu.VMEM((PAIRS, 2, sub, LANES), bf16),
            pltpu.VMEM((PAIRS, 2, rows, LANES), bf16),
            pltpu.VMEM((PAIRS, 2, out_rows, LANES), f32),
            pltpu.VMEM((PAIRS, out_rows, LANES), f32),
            pltpu.VMEM((PAIRS, 4, piece, LANES), f32),
            pltpu.VMEM((PAIRS, 4, piece, LANES), bf16),
            pltpu.VMEM((PAIRS, 3, piece, LANES), bf16),
            pltpu.VMEM((PAIRS, piece, LANES), bf16),
            pltpu.VMEM((4, piece, LANES), bf16),
            pltpu.VMEM((PAIRS, 2, out_rows, LANES), bf16),
            pltpu.VMEM((out_rows, rows), f32),
            dma((13 + rows // TILE,)),
            dma((PAIRS, 2, 19)),
            dma((PAIRS, 2, 19)),
            dma((PAIRS, 8)),
            dma((PAIRS, 8)),
            dma((3,)),
            dma((3,)),
            dma((7,)),
        ],
        compiler_params=pltpu.CompilerParams(
            collective_id=0, has_side_effects=True, vmem_limit_bytes=60 << 20
        ),
    )(eigvec, force_const, amplitudes, mlip_forces, frequency)


def last_kernel(grad, resid, disp, out):
    term = lax.dot_general(resid[...], disp[...], (((1,), (1,)), ((), ())), preferred_element_type=jnp.float32)
    out[...] = (grad[...] + term) * (1.0 / 32.0)


def add_last(grad, resid, disp):
    out_rows, rows = grad.shape
    configs = resid.shape[1]
    tile = out_rows // 6
    return pl.pallas_call(
        last_kernel,
        name="add_last",
        grid=(6,),
        out_shape=jax.ShapeDtypeStruct((out_rows, rows), jnp.float32),
        in_specs=[
            pl.BlockSpec((tile, rows), lambda i: (i, 0)),
            pl.BlockSpec((tile, configs), lambda i: (i, 0)),
            pl.BlockSpec((rows, configs), lambda i: (0, 0)),
        ],
        out_specs=pl.BlockSpec((tile, rows), lambda i: (i, 0)),
        compiler_params=pltpu.CompilerParams(vmem_limit_bytes=60 << 20),
    )(grad, resid, disp)


def local(eigvec, force_const, amplitudes, mlip_forces, frequency):
    return add_last(*exchange(eigvec.T, force_const, amplitudes, mlip_forces, frequency))


def solution(mesh):
    return jax.shard_map(
        local,
        mesh=mesh,
        in_specs=(
            P("row", ("col", "cfg")),
            P(("col", "cfg"), "row"),
            P(("col", "cfg"), None),
            P(("col", "cfg"), "row"),
            P(("col", "cfg")),
        ),
        out_specs=P(("col", "cfg"), "row"),
        check_vma=False,
    )
```

```python
import functools

import jax
import jax.numpy as jnp
from jax import lax
from jax.experimental import pallas as pl
from jax.experimental.pallas import tpu as pltpu
from jax.sharding import PartitionSpec as P

MESH = pl.DeviceIdType.MESH
PAIRS = 4
LANES = 128
TILE = 256
ORDER = [
    (0, 0), (0, 2), (1, 2, 0), (1, 2, 1), (0, 1), (1, 0, 1), (2, 2, 1), (1, 0, 0),
    (2, 2, 0), (1, 1, 1), (0, 3), (3, 2, 1), (2, 0, 1), (3, 2, 0), (2, 0, 0), (1, 1, 0),
    (1, 3, 1), (4, 2, 1), (4, 2, 0), (3, 0, 1), (2, 1, 1), (2, 1, 0), (1, 3, 0), (3, 0, 0),
    (5, 2, 1), (4, 0, 1), (5, 2, 0), (2, 3, 1), (3, 1, 1), (4, 0, 0), (2, 3, 0), (3, 1, 0),
    (6, 2, 1), (6, 2, 0), (5, 0, 1), (5, 0, 0), (4, 1, 0), (4, 1, 1), (3, 3, 1), (3, 3, 0),
    (7, 2), (6, 0, 1), (6, 0, 0), (4, 3, 0), (4, 3, 1), (8, 2), (5, 1, 0), (5, 1, 1),
    (7, 0), (6, 1, 1), (6, 1, 0), (8, 0), (5, 3, 1), (5, 3, 0), (9, 2, 1), (9, 2, 0),
    (7, 1), (6, 3, 1), (6, 3, 0), (9, 0, 0), (9, 0, 1), (8, 1), (7, 3), (10, 2),
    (8, 3), (11, 2), (10, 0), (9, 1, 0), (9, 1, 1), (11, 0), (12, 2, 0), (9, 3, 0),
    (9, 3, 1), (12, 0, 0), (12, 0, 1), (12, 2, 1), (10, 1), (12, 0, 2), (12, 2, 2), (11, 1),
    (12, 1, 0), (10, 3), (12, 1, 1), (12, 1, 2), (11, 3),
]


def comm_kernel(
    eig_hbm, fc_hbm, amp_hbm, forces_hbm, freq_ref, grad_hbm, resid_hbm, disp_hbm,
    eig_t, eig, fc, amp, scale, part32, part16, in_opp, in_near, sum32, sum16, in_second, own32, own16, in_zl,
    disp, harm, in_core, harm32, harm16, in_zh, force_in, force_own, resid, grad,
    load_sem, col_send, col_recv, row_send, row_recv, m_send, m_recv, out_sem,
):
    modes, rows = eig_hbm.shape
    quarter, sub = rows // 4, rows // 16
    half = quarter // 2
    out_rows = fc_hbm.shape[0]
    piece = out_rows // 4

    row, x, cfg = lax.axis_index("row"), lax.axis_index("col"), lax.axis_index("cfg")
    zh, core, y, zl = row // 2, row % 2, cfg // 2, cfg % 2

    def x_dev(d):
        return {"col": (x + d) % 4}

    def y_dev(d):
        return {"cfg": ((y + d) % 4) * 2 + zl}

    def zh_dev(d):
        return {"row": ((zh + d) % 4) * 2 + core}

    zl_dev = {"cfg": y * 2 + (1 - zl)}
    core_dev = {"row": zh * 2 + (1 - core)}
    axes = [(x, x_dev, y, y_dev), (y, y_dev, x, x_dev)]

    load_amp = [pltpu.make_async_copy(amp_hbm.at[:, pl.ds(p * 2 * LANES, 2 * LANES)], amp.at[p], load_sem.at[p]) for p in range(PAIRS)]
    load_eig = [pltpu.make_async_copy(eig_hbm.at[:, pl.ds(q * TILE, TILE)], eig_t.at[q], load_sem.at[13 + q]) for q in range(rows // TILE)]
    load_fc = pltpu.make_async_copy(fc_hbm, fc, load_sem.at[8])
    load_forces = [pltpu.make_async_copy(forces_hbm.at[pl.ds(q * piece, piece)], force_own.at[q], load_sem.at[9 + q]) for q in range(4)]
    for c in load_amp[:1] + load_eig + load_amp[1:] + load_forces + [load_fc]:
        c.start()

    barrier = pltpu.get_barrier_semaphore()
    peers = [x_dev(1), x_dev(2), x_dev(3), y_dev(1), y_dev(2), y_dev(3), zh_dev(1), zh_dev(2), zh_dev(3), zl_dev, core_dev]
    for dev in peers:
        pl.semaphore_signal(barrier, inc=1, device_id=dev, device_id_type=MESH)

    f = freq_ref[...].reshape(1, modes)
    on_diag = lax.broadcasted_iota(jnp.int32, (modes, modes), 0) == lax.broadcasted_iota(jnp.int32, (modes, modes), 1)
    f_col = jnp.sum(jnp.where(on_diag, f, 0.0), axis=1, keepdims=True)
    scale[...] = jnp.broadcast_to(1.0 / jnp.sqrt(2.0 * f_col), scale.shape)

    for q, c in enumerate(load_eig):
        c.wait()
        eig[pl.ds(q * TILE, TILE)] = eig_t[q].T
    load_amp[0].wait()

    def col_copy(p, t, k, src, dst, dev):
        return pltpu.make_async_remote_copy(
            src_ref=src, dst_ref=dst, send_sem=col_send.at[p, t, k], recv_sem=col_recv.at[p, t, k],
            device_id=dev, device_id_type=MESH,
        )

    def row_copy(p, k, src, dst, dev):
        return pltpu.make_async_remote_copy(
            src_ref=src, dst_ref=dst, send_sem=row_send.at[p, k], recv_sem=row_recv.at[p, k],
            device_id=dev, device_id_type=MESH,
        )

    lo, hi = pl.ds(0, half), pl.ds(half, half)

    def first_out(p, t, k):
        a, a_dev, _, _ = axes[t]
        q1, q2, q3 = (a + 1) % 4, (a + 2) % 4, (a + 3) % 4
        src, dst, dev = [
            (part16.at[p, t, q2, lo], in_opp.at[p, t, 0], 1),
            (part16.at[p, t, q2, hi], in_opp.at[p, t, 1], 3),
            (part16.at[p, t, q1, hi], in_near.at[p, t, 0, hi], 1),
            (part16.at[p, t, q3, lo], in_near.at[p, t, 1, lo], 3),
            (part16.at[p, t, q1, lo], in_near.at[p, t, 0, lo], 1),
            (part16.at[p, t, q3, hi], in_near.at[p, t, 1, hi], 3),
        ][k]
        return col_copy(p, t, k, src, dst, a_dev(dev))

    def second_out(p, t, d):
        _, _, b, b_dev = axes[t]
        return col_copy(p, t, 5 + d, sum16.at[p, t, (b + d) % 4], in_second.at[p, t, d - 1], b_dev(d))

    def zl_out(p, t):
        return col_copy(p, t, 9, own16.at[p, t], in_zl.at[p, t], zl_dev)

    def disp_at(p, t, start, size, align):
        return disp.at[p, t, pl.ds(pl.multiple_of(start, align), size)]

    def spread_b(p, t, d, owner):
        a, _, _, b_dev = axes[t]
        at = disp_at(p, t, a * quarter + owner * sub, sub, 16)
        return col_copy(p, t, 9 + d, at, at, b_dev(d))

    def spread_a(p, t, k, owner):
        _, a_dev, _, _ = axes[t]
        which, dev = [(0, 1), (1, 1), (1, 3), (0, 3), (0, 1), (1, 3)][k]
        at = disp_at(p, t, owner * quarter + which * half, half, 16)
        return col_copy(p, t, 13 + k, at, at, a_dev(dev))

    def core_out(p):
        return row_copy(p, 0, harm.at[p, 1 - core], in_core.at[p], core_dev)

    cut = piece // 32 * 16
    portions = [(0, piece - cut), (piece - cut, cut)]

    def zh_out(p, d, h):
        at = pl.ds(*portions[h])
        return row_copy(p, 2 * d - 1 + h, harm16.at[p, (zh + d) % 4, at], in_zh.at[p, d - 1, at], zh_dev(d))

    def resid_rows(owner, h):
        start, size = portions[h]
        return pl.ds(pl.multiple_of(owner * piece + start, 16), size)

    def resid_spread(p, d, h, owner):
        at = resid.at[p, core, resid_rows(owner, h)]
        return row_copy(p, 2 * d + 5 + h, at, at, zh_dev(d))

    def resid_core(p, which):
        at = resid.at[p, which]
        return row_copy(p, 13, at, at, core_dev)

    def disp_store(t):
        return pltpu.make_async_copy(disp.at[PAIRS - 1, t], disp_hbm.at[:, pl.ds(t * LANES, LANES)], out_sem.at[t])

    def resid_store(t):
        return pltpu.make_async_copy(resid.at[PAIRS - 1, t], resid_hbm.at[:, pl.ds(t * LANES, LANES)], out_sem.at[2 + t])

    def grad_store(g):
        at = pl.ds(g * 3 * TILE, 3 * TILE)
        return pltpu.make_async_copy(grad.at[:, at], grad_hbm.at[:, at], out_sem.at[4 + g])

    def force_out(d, slot):
        return pltpu.make_async_remote_copy(
            src_ref=force_own.at[(zh + d) % 4], dst_ref=force_in.at[slot],
            send_sem=m_send.at[d - 1], recv_sem=m_recv.at[d - 1], device_id=zh_dev(d), device_id_type=MESH,
        )

    def first_part():
        scaled = (scale[:, :1] * amp[0].astype(jnp.float32)).astype(jnp.bfloat16)

        def one(t, d):
            q = (axes[t][0] + d) % 4
            block = jnp.dot(
                eig[pl.ds(pl.multiple_of(q * quarter, 16), quarter)],
                scaled[:, t * LANES : (t + 1) * LANES],
                preferred_element_type=jnp.float32,
            )
            part32[0, t, q] = block
            part16[0, t, q] = block.astype(jnp.bfloat16)

        for t in range(2):
            one(t, 2)
        pl.semaphore_wait(barrier, len(peers))
        for k in range(2):
            for t in range(2):
                first_out(0, t, k).start()
        for d, k in ((1, 2), (3, 3)):
            for t in range(2):
                one(t, d)
                first_out(0, t, k).start()
        for t in range(2):
            one(t, 0)

    def compute_part(p):
        load_amp[p].wait()
        scaled = (scale[:, :1] * amp[p].astype(jnp.float32)).astype(jnp.bfloat16)

        def one(q, carry):
            product = jnp.dot(eig[pl.ds(pl.multiple_of(q * quarter, 16), quarter)], scaled, preferred_element_type=jnp.float32)
            for t in range(2):
                block = product[:, t * LANES : (t + 1) * LANES]
                part32[p, t, q] = block
                part16[p, t, q] = block.astype(jnp.bfloat16)
            return carry

        lax.fori_loop(0, 4, one, 0)

    def send_part(p):
        for k in range(4):
            for t in range(2):
                first_out(p, t, k).start()

    harm_first = [step[1] for step in ORDER if step[0] == 7][0]
    grad_pairs = [[step[1] for step in ORDER if step[0] == 12 and step[2] == g] for g in range(3)]

    def stage0(p):
        if p == 0:
            first_part()
            for c in load_forces:
                c.wait()
            force_in[zh] = force_own[zh]
            for d in (1, 2, 3):
                force_out(d, zh).start()
        else:
            compute_part(p)
            send_part(p)

    def stage1(p, t):
        a = axes[t][0]
        first_out(p, t, 0).wait_recv()
        q1, q3 = (a + 1) % 4, (a + 3) % 4
        part16[p, t, q1, lo] = (part32[p, t, q1, lo] + in_opp[p, t, 0].astype(jnp.float32)).astype(jnp.bfloat16)
        first_out(p, t, 4).start()
        first_out(p, t, 1).wait_recv()
        part16[p, t, q3, hi] = (part32[p, t, q3, hi] + in_opp[p, t, 1].astype(jnp.float32)).astype(jnp.bfloat16)
        first_out(p, t, 5).start()

    def stage2(p, t):
        a, _, b, _ = axes[t]
        for k in range(2, 6):
            first_out(p, t, k).wait_recv()
        total = part32[p, t, a] + in_near[p, t, 0].astype(jnp.float32) + in_near[p, t, 1].astype(jnp.float32)
        total = total.reshape(4, sub, LANES)
        sum32[p, t] = total
        sum16[p, t] = total.astype(jnp.bfloat16)
        for d in (2, 1, 3):
            second_out(p, t, d).start()

    def stage3(p, t):
        b = axes[t][2]
        for d in (1, 2, 3):
            second_out(p, t, d).wait_recv()
        total = sum32[p, t, b]
        for d in range(3):
            total += in_second[p, t, d].astype(jnp.float32)
        own32[p, t] = total
        own16[p, t] = total.astype(jnp.bfloat16)
        zl_out(p, t).start()

    def stage4(p, t):
        a, _, b, _ = axes[t]
        zl_out(p, t).wait_recv()
        value = (own32[p, t] + in_zl[p, t].astype(jnp.float32)).astype(jnp.bfloat16)
        disp[p, t, pl.ds(pl.multiple_of(a * quarter + b * sub, 16), sub)] = value
        for d in (2, 1, 3):
            spread_b(p, t, d, b).start()

    def stage5(p, t):
        a, _, b, _ = axes[t]
        for d in (1, 2, 3):
            spread_b(p, t, d, (b + 4 - d) % 4).wait_recv()
        for k in (0, 2, 1, 3):
            spread_a(p, t, k, a).start()

    def stage6(p, t):
        a = axes[t][0]
        below, above = (a + 3) % 4, (a + 1) % 4
        spread_a(p, t, 0, below).wait_recv()
        spread_a(p, t, 4, below).start()
        spread_a(p, t, 2, above).wait_recv()
        spread_a(p, t, 5, above).start()

    def stage7(p):
        for t in range(2):
            a = axes[t][0]
            below, above, far = (a + 3) % 4, (a + 1) % 4, (a + 2) % 4
            spread_a(p, t, 1, below).wait_recv()
            spread_a(p, t, 3, above).wait_recv()
            spread_a(p, t, 4, far).wait_recv()
            spread_a(p, t, 5, far).wait_recv()
        if p == PAIRS - 1:
            for t in range(2):
                disp_store(t).start()
        if p == harm_first:
            load_fc.wait()
            for d in (1, 2, 3):
                force_out(d, (zh + 4 - d) % 4).wait_recv()

        product = jnp.dot(fc[...], jnp.concatenate([disp[p, 0], disp[p, 1]], axis=1), preferred_element_type=jnp.float32)
        for t in range(2):
            harm[p, t] = product[:, t * LANES : (t + 1) * LANES]
        core_out(p).start()

    def stage8(p):
        core_out(p).wait_recv()
        total = (harm[p, core] + in_core[p]).reshape(4, piece, LANES)
        harm32[p] = total
        harm16[p] = total.astype(jnp.bfloat16)
        for h in range(2):
            for d in (2, 1, 3):
                zh_out(p, d, h).start()

    def stage9(p, h):
        for d in (1, 2, 3):
            zh_out(p, d, h).wait_recv()
        at = pl.ds(*portions[h])
        total = force_in[p, at].astype(jnp.float32) + harm32[p, zh, at]
        for d in range(3):
            total += in_zh[p, d, at].astype(jnp.float32)
        resid[p, core, resid_rows(zh, h)] = total.astype(jnp.bfloat16)
        for d in (2, 1, 3):
            resid_spread(p, d, h, zh).start()

    def stage10(p):
        for h in range(2):
            for d in (1, 2, 3):
                resid_spread(p, d, h, (zh + 4 - d) % 4).wait_recv()
        resid_core(p, core).start()

    def stage11(p):
        resid_core(p, 1 - core).wait_recv()
        if p == PAIRS - 1:
            for t in range(2):
                resid_store(t).start()

    def stage12(p, g):
        left = jnp.concatenate([resid[p, 0], resid[p, 1]], axis=1)
        for c in range(g * 3, g * 3 + 3):
            at = pl.ds(c * TILE, TILE)
            right = jnp.concatenate([disp[p, 0, at], disp[p, 1, at]], axis=1)
            term = lax.dot_general(left, right, (((1,), (1,)), ((), ())), preferred_element_type=jnp.float32)
            if p != grad_pairs[g][0]:
                term += grad[:, at]
            grad[:, at] = term
        if p == grad_pairs[g][-1]:
            grad_store(g).start()

    stages = [stage0, stage1, stage2, stage3, stage4, stage5, stage6, stage7, stage8, stage9, stage10, stage11, stage12]
    for s, *which in ORDER:
        stages[s](*which)

    def drain(p, carry):
        for t in range(2):
            a, _, b, _ = axes[t]
            for k in range(6):
                first_out(p, t, k).wait_send()
                spread_a(p, t, k, a).wait_send()
            for d in (1, 2, 3):
                second_out(p, t, d).wait_send()
                spread_b(p, t, d, b).wait_send()
            zl_out(p, t).wait_send()
        core_out(p).wait_send()
        for h in range(2):
            for d in (1, 2, 3):
                zh_out(p, d, h).wait_send()
                resid_spread(p, d, h, zh).wait_send()
        resid_core(p, core).wait_send()
        return carry

    lax.fori_loop(0, PAIRS, drain, 0)
    for t in range(2):
        disp_store(t).wait()
        resid_store(t).wait()
    for g in range(3):
        grad_store(g).wait()
    for d in (1, 2, 3):
        force_out(d, zh).wait_send()


def exchange(eigvec, force_const, amplitudes, mlip_forces, frequency):
    modes, rows = eigvec.shape
    out_rows = force_const.shape[0]
    quarter, sub, piece = rows // 4, rows // 16, out_rows // 4
    half = quarter // 2
    bf16, f32 = jnp.bfloat16, jnp.float32
    anywhere = pl.BlockSpec(memory_space=pl.ANY)
    dma = pltpu.SemaphoreType.DMA
    return pl.pallas_call(
        comm_kernel,
        name="exchange",
        out_shape=[
            jax.ShapeDtypeStruct((out_rows, rows), f32),
            jax.ShapeDtypeStruct((out_rows, 2 * LANES), bf16),
            jax.ShapeDtypeStruct((rows, 2 * LANES), bf16),
        ],
        in_specs=[anywhere] * 4 + [pl.BlockSpec(memory_space=pltpu.VMEM)],
        out_specs=[anywhere] * 3,
        scratch_shapes=[
            pltpu.VMEM((rows // TILE, modes, TILE), bf16),
            pltpu.VMEM((rows, modes), bf16),
            pltpu.VMEM((out_rows, rows), bf16),
            pltpu.VMEM((PAIRS, modes, 2 * LANES), bf16),
            pltpu.VMEM((modes, LANES), f32),
            pltpu.VMEM((PAIRS, 2, 4, quarter, LANES), f32),
            pltpu.VMEM((PAIRS, 2, 4, quarter, LANES), bf16),
            pltpu.VMEM((PAIRS, 2, 2, half, LANES), bf16),
            pltpu.VMEM((PAIRS, 2, 2, quarter, LANES), bf16),
            pltpu.VMEM((PAIRS, 2, 4, sub, LANES), f32),
            pltpu.VMEM((PAIRS, 2, 4, sub, LANES), bf16),
            pltpu.VMEM((PAIRS, 2, 3, sub, LANES), bf16),
            pltpu.VMEM((PAIRS, 2, sub, LANES), f32),
            pltpu.VMEM((PAIRS, 2, sub, LANES), bf16),
            pltpu.VMEM((PAIRS, 2, sub, LANES), bf16),
            pltpu.VMEM((PAIRS, 2, rows, LANES), bf16),
            pltpu.VMEM((PAIRS, 2, out_rows, LANES), f32),
            pltpu.VMEM((PAIRS, out_rows, LANES), f32),
            pltpu.VMEM((PAIRS, 4, piece, LANES), f32),
            pltpu.VMEM((PAIRS, 4, piece, LANES), bf16),
            pltpu.VMEM((PAIRS, 3, piece, LANES), bf16),
            pltpu.VMEM((PAIRS, piece, LANES), bf16),
            pltpu.VMEM((4, piece, LANES), bf16),
            pltpu.VMEM((PAIRS, 2, out_rows, LANES), bf16),
            pltpu.VMEM((out_rows, rows), f32),
            dma((13 + rows // TILE,)),
            dma((PAIRS, 2, 19)),
            dma((PAIRS, 2, 19)),
            dma((PAIRS, 14)),
            dma((PAIRS, 14)),
            dma((3,)),
            dma((3,)),
            dma((7,)),
        ],
        compiler_params=pltpu.CompilerParams(
            collective_id=0, has_side_effects=True, vmem_limit_bytes=60 << 20
        ),
    )(eigvec, force_const, amplitudes, mlip_forces, frequency)


def last_kernel(grad_hbm, resid_hbm, disp_hbm, out_hbm, grad, resid, disp, total, load_sem, store_sem):
    tiles = disp.shape[0] // TILE

    def load_grad(c):
        at = pl.ds(c * TILE, TILE)
        return pltpu.make_async_copy(grad_hbm.at[:, at], grad.at[:, at], load_sem.at[c])

    def store(c):
        at = pl.ds(c * TILE, TILE)
        return pltpu.make_async_copy(total.at[:, at], out_hbm.at[:, at], store_sem.at[c])

    load_resid = pltpu.make_async_copy(resid_hbm, resid, load_sem.at[tiles])
    load_disp = pltpu.make_async_copy(disp_hbm, disp, load_sem.at[tiles + 1])
    load_resid.start()
    load_disp.start()
    for c in range(tiles):
        load_grad(c).start()
    load_resid.wait()
    load_disp.wait()
    for c in range(tiles):
        at = pl.ds(c * TILE, TILE)
        term = lax.dot_general(resid[...], disp[at], (((1,), (1,)), ((), ())), preferred_element_type=jnp.float32)
        load_grad(c).wait()
        total[:, at] = (grad[:, at] + term) * (1.0 / 32.0)
        store(c).start()
    for c in range(tiles):
        store(c).wait()


def add_last(grad, resid, disp):
    anywhere = pl.BlockSpec(memory_space=pl.ANY)
    tiles = disp.shape[0] // TILE
    return pl.pallas_call(
        last_kernel,
        name="add_last",
        out_shape=jax.ShapeDtypeStruct(grad.shape, jnp.float32),
        in_specs=[anywhere] * 3,
        out_specs=anywhere,
        scratch_shapes=[
            pltpu.VMEM(grad.shape, jnp.float32),
            pltpu.VMEM(resid.shape, jnp.bfloat16),
            pltpu.VMEM(disp.shape, jnp.bfloat16),
            pltpu.VMEM(grad.shape, jnp.float32),
            pltpu.SemaphoreType.DMA((tiles + 2,)),
            pltpu.SemaphoreType.DMA((tiles,)),
        ],
        compiler_params=pltpu.CompilerParams(vmem_limit_bytes=60 << 20),
    )(grad, resid, disp)


def local(eigvec, force_const, amplitudes, mlip_forces, frequency):
    return add_last(*exchange(eigvec.T, force_const, amplitudes, mlip_forces, frequency))


def solution(mesh):
    return jax.shard_map(
        local,
        mesh=mesh,
        in_specs=(
            P("row", ("col", "cfg")),
            P(("col", "cfg"), "row"),
            P(("col", "cfg"), None),
            P(("col", "cfg"), "row"),
            P(("col", "cfg")),
        ),
        out_specs=P(("col", "cfg"), "row"),
        check_vma=False,
    )
```

```python
import functools

import jax
import jax.numpy as jnp
from jax import lax
from jax.experimental import pallas as pl
from jax.experimental.pallas import tpu as pltpu
from jax.sharding import PartitionSpec as P

MESH = pl.DeviceIdType.MESH
PAIRS = 4
LANES = 128
TILE = 256
ORDER = [
    (0, 0), (0, 1), (1, 0, 1), (1, 0, 0), (0, 3), (1, 1, 0), (1, 1, 1), (2, 0, 0),
    (2, 0, 1), (0, 2), (2, 1, 0), (2, 1, 1), (3, 0, 1), (3, 0, 0), (1, 2, 0), (1, 2, 1),
    (1, 3, 1), (4, 0, 1), (1, 3, 0), (4, 0, 0), (3, 1, 1), (3, 1, 0), (2, 2, 0), (2, 2, 1),
    (5, 0, 1), (4, 1, 1), (5, 0, 0), (4, 1, 0), (2, 3, 1), (3, 2, 1), (2, 3, 0), (6, 0, 1),
    (3, 2, 0), (5, 1, 1), (6, 0, 0), (5, 1, 0), (4, 2, 1), (3, 3, 0), (3, 3, 1), (4, 2, 0),
    (7, 0), (6, 1, 0), (6, 1, 1), (4, 3, 1), (4, 3, 0), (5, 2, 0), (5, 2, 1), (8, 0),
    (7, 1), (6, 2, 0), (6, 2, 1), (5, 3, 0), (8, 1), (5, 3, 1), (9, 0, 0), (7, 2),
    (6, 3, 0), (6, 3, 1), (9, 0, 1), (9, 1, 0), (9, 1, 1), (8, 2), (7, 3), (10, 0),
    (8, 3), (11, 0), (10, 1), (12, 0, 0), (9, 2, 0), (12, 0, 1), (9, 2, 1), (11, 1),
    (12, 1, 0), (9, 3, 0), (9, 3, 1), (12, 0, 2), (12, 1, 1), (10, 2), (12, 1, 2), (11, 2),
    (12, 2, 0), (10, 3), (12, 2, 1), (12, 2, 2), (11, 3),
]


def comm_kernel(
    eig_hbm, fc_hbm, amp_hbm, forces_hbm, freq_ref, grad_hbm, resid_hbm, disp_hbm,
    eig_t, eig, fc, amp, scale, part32, part16, in_opp, in_near, sum32, sum16, in_second, own32, own16, in_zl,
    disp, harm, in_core, harm32, harm16, in_zh, force_in, force_own, resid, grad,
    load_sem, col_send, col_recv, row_send, row_recv, m_send, m_recv, out_sem,
):
    modes, rows = eig_hbm.shape
    quarter, sub = rows // 4, rows // 16
    half = quarter // 2
    out_rows = fc_hbm.shape[0]
    piece = out_rows // 4

    row, x, cfg = lax.axis_index("row"), lax.axis_index("col"), lax.axis_index("cfg")
    zh, core, y, zl = row // 2, row % 2, cfg // 2, cfg % 2

    def x_dev(d):
        return {"col": (x + d) % 4}

    def y_dev(d):
        return {"cfg": ((y + d) % 4) * 2 + zl}

    def zh_dev(d):
        return {"row": ((zh + d) % 4) * 2 + core}

    zl_dev = {"cfg": y * 2 + (1 - zl)}
    core_dev = {"row": zh * 2 + (1 - core)}
    axes = [(x, x_dev, y, y_dev), (y, y_dev, x, x_dev)]

    load_amp = [pltpu.make_async_copy(amp_hbm.at[:, pl.ds(p * 2 * LANES, 2 * LANES)], amp.at[p], load_sem.at[p]) for p in range(PAIRS)]
    load_eig = [pltpu.make_async_copy(eig_hbm.at[:, pl.ds(q * TILE, TILE)], eig_t.at[q], load_sem.at[13 + q]) for q in range(rows // TILE)]
    load_fc = pltpu.make_async_copy(fc_hbm, fc, load_sem.at[8])
    load_forces = [pltpu.make_async_copy(forces_hbm.at[pl.ds(q * piece, piece)], force_own.at[q], load_sem.at[9 + q]) for q in range(4)]
    for c in load_amp[:1] + load_eig:
        c.start()

    barrier = pltpu.get_barrier_semaphore()
    peers = [x_dev(1), x_dev(2), x_dev(3), y_dev(1), y_dev(2), y_dev(3), zh_dev(1), zh_dev(2), zh_dev(3), zl_dev, core_dev]
    for dev in peers:
        pl.semaphore_signal(barrier, inc=1, device_id=dev, device_id_type=MESH)

    f = freq_ref[...].reshape(1, modes)
    on_diag = lax.broadcasted_iota(jnp.int32, (modes, modes), 0) == lax.broadcasted_iota(jnp.int32, (modes, modes), 1)
    f_col = jnp.sum(jnp.where(on_diag, f, 0.0), axis=1, keepdims=True)
    scale[...] = jnp.broadcast_to(1.0 / jnp.sqrt(2.0 * f_col), scale.shape)

    for q, c in enumerate(load_eig):
        c.wait()
        eig[pl.ds(q * TILE, TILE)] = eig_t[q].T
    for c in load_amp[1:] + load_forces + [load_fc]:
        c.start()
    load_amp[0].wait()

    def col_copy(p, t, k, src, dst, dev):
        return pltpu.make_async_remote_copy(
            src_ref=src, dst_ref=dst, send_sem=col_send.at[p, t, k], recv_sem=col_recv.at[p, t, k],
            device_id=dev, device_id_type=MESH,
        )

    def row_copy(p, k, src, dst, dev):
        return pltpu.make_async_remote_copy(
            src_ref=src, dst_ref=dst, send_sem=row_send.at[p, k], recv_sem=row_recv.at[p, k],
            device_id=dev, device_id_type=MESH,
        )

    lo, hi = pl.ds(0, half), pl.ds(half, half)

    def first_out(p, t, k):
        a, a_dev, _, _ = axes[t]
        q1, q2, q3 = (a + 1) % 4, (a + 2) % 4, (a + 3) % 4
        src, dst, dev = [
            (part16.at[p, t, q2, lo], in_opp.at[p, t, 0], 1),
            (part16.at[p, t, q2, hi], in_opp.at[p, t, 1], 3),
            (part16.at[p, t, q1, hi], in_near.at[p, t, 0, hi], 1),
            (part16.at[p, t, q3, lo], in_near.at[p, t, 1, lo], 3),
            (part16.at[p, t, q1, lo], in_near.at[p, t, 0, lo], 1),
            (part16.at[p, t, q3, hi], in_near.at[p, t, 1, hi], 3),
        ][k]
        return col_copy(p, t, k, src, dst, a_dev(dev))

    def second_out(p, t, d):
        _, _, b, b_dev = axes[t]
        return col_copy(p, t, 5 + d, sum16.at[p, t, (b + d) % 4], in_second.at[p, t, d - 1], b_dev(d))

    def zl_out(p, t):
        return col_copy(p, t, 9, own16.at[p, t], in_zl.at[p, t], zl_dev)

    def disp_at(p, t, start, size, align):
        return disp.at[p, t, pl.ds(pl.multiple_of(start, align), size)]

    def spread_b(p, t, d, owner):
        a, _, _, b_dev = axes[t]
        at = disp_at(p, t, a * quarter + owner * sub, sub, 16)
        return col_copy(p, t, 9 + d, at, at, b_dev(d))

    def spread_a(p, t, k, owner):
        _, a_dev, _, _ = axes[t]
        which, dev = [(0, 1), (1, 1), (1, 3), (0, 3), (0, 1), (1, 3)][k]
        at = disp_at(p, t, owner * quarter + which * half, half, 16)
        return col_copy(p, t, 13 + k, at, at, a_dev(dev))

    def core_out(p):
        return row_copy(p, 0, harm.at[p, 1 - core], in_core.at[p], core_dev)

    cut = piece // 32 * 16
    portions = [(0, piece - cut), (piece - cut, cut)]

    def zh_out(p, d, h):
        at = pl.ds(*portions[h])
        return row_copy(p, 2 * d - 1 + h, harm16.at[p, (zh + d) % 4, at], in_zh.at[p, d - 1, at], zh_dev(d))

    def resid_rows(owner, h):
        start, size = portions[h]
        return pl.ds(pl.multiple_of(owner * piece + start, 16), size)

    def resid_spread(p, d, h, owner):
        at = resid.at[p, core, resid_rows(owner, h)]
        return row_copy(p, 2 * d + 5 + h, at, at, zh_dev(d))

    def resid_core(p, which):
        at = resid.at[p, which]
        return row_copy(p, 13, at, at, core_dev)

    def disp_store(t):
        return pltpu.make_async_copy(disp.at[PAIRS - 1, t], disp_hbm.at[:, pl.ds(t * LANES, LANES)], out_sem.at[t])

    def resid_store(t):
        return pltpu.make_async_copy(resid.at[PAIRS - 1, t], resid_hbm.at[:, pl.ds(t * LANES, LANES)], out_sem.at[2 + t])

    def grad_store(g):
        at = pl.ds(g * 3 * TILE, 3 * TILE)
        return pltpu.make_async_copy(grad.at[:, at], grad_hbm.at[:, at], out_sem.at[4 + g])

    def force_out(d, slot):
        return pltpu.make_async_remote_copy(
            src_ref=force_own.at[(zh + d) % 4], dst_ref=force_in.at[slot],
            send_sem=m_send.at[d - 1], recv_sem=m_recv.at[d - 1], device_id=zh_dev(d), device_id_type=MESH,
        )

    def first_part():
        scaled = (scale[:, :1] * amp[0].astype(jnp.float32)).astype(jnp.bfloat16)

        def one(t, d):
            q = (axes[t][0] + d) % 4
            block = jnp.dot(
                eig[pl.ds(pl.multiple_of(q * quarter, 16), quarter)],
                scaled[:, t * LANES : (t + 1) * LANES],
                preferred_element_type=jnp.float32,
            )
            part32[0, t, q] = block
            part16[0, t, q] = block.astype(jnp.bfloat16)

        for t in range(2):
            one(t, 2)
        pl.semaphore_wait(barrier, len(peers))
        for k in range(2):
            for t in range(2):
                first_out(0, t, k).start()
        for d, k in ((1, 2), (3, 3)):
            for t in range(2):
                one(t, d)
                first_out(0, t, k).start()
        for t in range(2):
            one(t, 0)

    def compute_part(p):
        load_amp[p].wait()
        scaled = (scale[:, :1] * amp[p].astype(jnp.float32)).astype(jnp.bfloat16)

        def one(q, carry):
            product = jnp.dot(eig[pl.ds(pl.multiple_of(q * quarter, 16), quarter)], scaled, preferred_element_type=jnp.float32)
            for t in range(2):
                block = product[:, t * LANES : (t + 1) * LANES]
                part32[p, t, q] = block
                part16[p, t, q] = block.astype(jnp.bfloat16)
            return carry

        lax.fori_loop(0, 4, one, 0)

    def send_part(p):
        for k in range(4):
            for t in range(2):
                first_out(p, t, k).start()

    harm_first = [step[1] for step in ORDER if step[0] == 7][0]
    grad_pairs = [[step[1] for step in ORDER if step[0] == 12 and step[2] == g] for g in range(3)]

    def stage0(p):
        if p == 0:
            first_part()
            for c in load_forces:
                c.wait()
            force_in[zh] = force_own[zh]
            for d in (1, 2, 3):
                force_out(d, zh).start()
        else:
            compute_part(p)
            send_part(p)

    def stage1(p, t):
        a = axes[t][0]
        first_out(p, t, 0).wait_recv()
        q1, q3 = (a + 1) % 4, (a + 3) % 4
        part16[p, t, q1, lo] = (part32[p, t, q1, lo] + in_opp[p, t, 0].astype(jnp.float32)).astype(jnp.bfloat16)
        first_out(p, t, 4).start()
        first_out(p, t, 1).wait_recv()
        part16[p, t, q3, hi] = (part32[p, t, q3, hi] + in_opp[p, t, 1].astype(jnp.float32)).astype(jnp.bfloat16)
        first_out(p, t, 5).start()

    def stage2(p, t):
        a, _, b, _ = axes[t]
        for k in range(2, 6):
            first_out(p, t, k).wait_recv()
        total = part32[p, t, a] + in_near[p, t, 0].astype(jnp.float32) + in_near[p, t, 1].astype(jnp.float32)
        total = total.reshape(4, sub, LANES)
        sum32[p, t] = total
        sum16[p, t] = total.astype(jnp.bfloat16)
        for d in (2, 1, 3):
            second_out(p, t, d).start()

    def stage3(p, t):
        b = axes[t][2]
        for d in (1, 2, 3):
            second_out(p, t, d).wait_recv()
        total = sum32[p, t, b]
        for d in range(3):
            total += in_second[p, t, d].astype(jnp.float32)
        own32[p, t] = total
        own16[p, t] = total.astype(jnp.bfloat16)
        zl_out(p, t).start()

    def stage4(p, t):
        a, _, b, _ = axes[t]
        zl_out(p, t).wait_recv()
        value = (own32[p, t] + in_zl[p, t].astype(jnp.float32)).astype(jnp.bfloat16)
        disp[p, t, pl.ds(pl.multiple_of(a * quarter + b * sub, 16), sub)] = value
        for d in (2, 1, 3):
            spread_b(p, t, d, b).start()

    def stage5(p, t):
        a, _, b, _ = axes[t]
        for d in (1, 2, 3):
            spread_b(p, t, d, (b + 4 - d) % 4).wait_recv()
        for k in (0, 2, 1, 3):
            spread_a(p, t, k, a).start()

    def stage6(p, t):
        a = axes[t][0]
        below, above = (a + 3) % 4, (a + 1) % 4
        spread_a(p, t, 0, below).wait_recv()
        spread_a(p, t, 4, below).start()
        spread_a(p, t, 2, above).wait_recv()
        spread_a(p, t, 5, above).start()

    def stage7(p):
        for t in range(2):
            a = axes[t][0]
            below, above, far = (a + 3) % 4, (a + 1) % 4, (a + 2) % 4
            spread_a(p, t, 1, below).wait_recv()
            spread_a(p, t, 3, above).wait_recv()
            spread_a(p, t, 4, far).wait_recv()
            spread_a(p, t, 5, far).wait_recv()
        if p == PAIRS - 1:
            for t in range(2):
                disp_store(t).start()
        if p == harm_first:
            load_fc.wait()
            for d in (1, 2, 3):
                force_out(d, (zh + 4 - d) % 4).wait_recv()

        product = jnp.dot(fc[...], jnp.concatenate([disp[p, 0], disp[p, 1]], axis=1), preferred_element_type=jnp.float32)
        for t in range(2):
            harm[p, t] = product[:, t * LANES : (t + 1) * LANES]
        core_out(p).start()

    def stage8(p):
        core_out(p).wait_recv()
        total = (harm[p, core] + in_core[p]).reshape(4, piece, LANES)
        harm32[p] = total
        harm16[p] = total.astype(jnp.bfloat16)
        for h in range(2):
            for d in (2, 1, 3):
                zh_out(p, d, h).start()

    def stage9(p, h):
        for d in (1, 2, 3):
            zh_out(p, d, h).wait_recv()
        at = pl.ds(*portions[h])
        total = force_in[p, at].astype(jnp.float32) + harm32[p, zh, at]
        for d in range(3):
            total += in_zh[p, d, at].astype(jnp.float32)
        resid[p, core, resid_rows(zh, h)] = total.astype(jnp.bfloat16)
        for d in (2, 1, 3):
            resid_spread(p, d, h, zh).start()

    def stage10(p):
        for h in range(2):
            for d in (1, 2, 3):
                resid_spread(p, d, h, (zh + 4 - d) % 4).wait_recv()
        resid_core(p, core).start()

    def stage11(p):
        resid_core(p, 1 - core).wait_recv()
        if p == PAIRS - 1:
            for t in range(2):
                resid_store(t).start()

    def stage12(p, g):
        left = jnp.concatenate([resid[p, 0], resid[p, 1]], axis=1)
        for c in range(g * 3, g * 3 + 3):
            at = pl.ds(c * TILE, TILE)
            right = jnp.concatenate([disp[p, 0, at], disp[p, 1, at]], axis=1)
            term = lax.dot_general(left, right, (((1,), (1,)), ((), ())), preferred_element_type=jnp.float32)
            if p != grad_pairs[g][0]:
                term += grad[:, at]
            grad[:, at] = term
        if p == grad_pairs[g][-1]:
            grad_store(g).start()

    stages = [stage0, stage1, stage2, stage3, stage4, stage5, stage6, stage7, stage8, stage9, stage10, stage11, stage12]
    for s, *which in ORDER:
        stages[s](*which)

    def drain(p, carry):
        for t in range(2):
            a, _, b, _ = axes[t]
            for k in range(6):
                first_out(p, t, k).wait_send()
                spread_a(p, t, k, a).wait_send()
            for d in (1, 2, 3):
                second_out(p, t, d).wait_send()
                spread_b(p, t, d, b).wait_send()
            zl_out(p, t).wait_send()
        core_out(p).wait_send()
        for h in range(2):
            for d in (1, 2, 3):
                zh_out(p, d, h).wait_send()
                resid_spread(p, d, h, zh).wait_send()
        resid_core(p, core).wait_send()
        return carry

    lax.fori_loop(0, PAIRS, drain, 0)
    for t in range(2):
        disp_store(t).wait()
        resid_store(t).wait()
    for g in range(3):
        grad_store(g).wait()
    for d in (1, 2, 3):
        force_out(d, zh).wait_send()


def exchange(eigvec, force_const, amplitudes, mlip_forces, frequency):
    modes, rows = eigvec.shape
    out_rows = force_const.shape[0]
    quarter, sub, piece = rows // 4, rows // 16, out_rows // 4
    half = quarter // 2
    bf16, f32 = jnp.bfloat16, jnp.float32
    anywhere = pl.BlockSpec(memory_space=pl.ANY)
    dma = pltpu.SemaphoreType.DMA
    return pl.pallas_call(
        comm_kernel,
        name="exchange",
        out_shape=[
            jax.ShapeDtypeStruct((out_rows, rows), f32),
            jax.ShapeDtypeStruct((out_rows, 2 * LANES), bf16),
            jax.ShapeDtypeStruct((rows, 2 * LANES), bf16),
        ],
        in_specs=[anywhere] * 4 + [pl.BlockSpec(memory_space=pltpu.VMEM)],
        out_specs=[anywhere] * 3,
        scratch_shapes=[
            pltpu.VMEM((rows // TILE, modes, TILE), bf16),
            pltpu.VMEM((rows, modes), bf16),
            pltpu.VMEM((out_rows, rows), bf16),
            pltpu.VMEM((PAIRS, modes, 2 * LANES), bf16),
            pltpu.VMEM((modes, LANES), f32),
            pltpu.VMEM((PAIRS, 2, 4, quarter, LANES), f32),
            pltpu.VMEM((PAIRS, 2, 4, quarter, LANES), bf16),
            pltpu.VMEM((PAIRS, 2, 2, half, LANES), bf16),
            pltpu.VMEM((PAIRS, 2, 2, quarter, LANES), bf16),
            pltpu.VMEM((PAIRS, 2, 4, sub, LANES), f32),
            pltpu.VMEM((PAIRS, 2, 4, sub, LANES), bf16),
            pltpu.VMEM((PAIRS, 2, 3, sub, LANES), bf16),
            pltpu.VMEM((PAIRS, 2, sub, LANES), f32),
            pltpu.VMEM((PAIRS, 2, sub, LANES), bf16),
            pltpu.VMEM((PAIRS, 2, sub, LANES), bf16),
            pltpu.VMEM((PAIRS, 2, rows, LANES), bf16),
            pltpu.VMEM((PAIRS, 2, out_rows, LANES), f32),
            pltpu.VMEM((PAIRS, out_rows, LANES), f32),
            pltpu.VMEM((PAIRS, 4, piece, LANES), f32),
            pltpu.VMEM((PAIRS, 4, piece, LANES), bf16),
            pltpu.VMEM((PAIRS, 3, piece, LANES), bf16),
            pltpu.VMEM((PAIRS, piece, LANES), bf16),
            pltpu.VMEM((4, piece, LANES), bf16),
            pltpu.VMEM((PAIRS, 2, out_rows, LANES), bf16),
            pltpu.VMEM((out_rows, rows), f32),
            dma((13 + rows // TILE,)),
            dma((PAIRS, 2, 19)),
            dma((PAIRS, 2, 19)),
            dma((PAIRS, 14)),
            dma((PAIRS, 14)),
            dma((3,)),
            dma((3,)),
            dma((7,)),
        ],
        compiler_params=pltpu.CompilerParams(
            collective_id=0, has_side_effects=True, vmem_limit_bytes=60 << 20
        ),
    )(eigvec, force_const, amplitudes, mlip_forces, frequency)


def last_kernel(grad_hbm, resid_hbm, disp_hbm, out_hbm, grad, resid, disp, total, load_sem, store_sem):
    tiles = disp.shape[0] // TILE

    def load_grad(c):
        at = pl.ds(c * TILE, TILE)
        return pltpu.make_async_copy(grad_hbm.at[:, at], grad.at[:, at], load_sem.at[c])

    def store(c):
        at = pl.ds(c * TILE, TILE)
        return pltpu.make_async_copy(total.at[:, at], out_hbm.at[:, at], store_sem.at[c])

    load_resid = pltpu.make_async_copy(resid_hbm, resid, load_sem.at[tiles])

    def load_disp(c):
        at = pl.ds(c * TILE, TILE)
        return pltpu.make_async_copy(disp_hbm.at[at], disp.at[at], load_sem.at[tiles + 1 + c])

    load_resid.start()
    for c in range(tiles):
        load_disp(c).start()
        load_grad(c).start()
    load_resid.wait()
    for c in range(tiles):
        at = pl.ds(c * TILE, TILE)
        load_disp(c).wait()
        term = lax.dot_general(resid[...], disp[at], (((1,), (1,)), ((), ())), preferred_element_type=jnp.float32)
        load_grad(c).wait()
        total[:, at] = (grad[:, at] + term) * (1.0 / 32.0)
        store(c).start()
    for c in range(tiles):
        store(c).wait()


def add_last(grad, resid, disp):
    anywhere = pl.BlockSpec(memory_space=pl.ANY)
    tiles = disp.shape[0] // TILE
    return pl.pallas_call(
        last_kernel,
        name="add_last",
        out_shape=jax.ShapeDtypeStruct(grad.shape, jnp.float32),
        in_specs=[anywhere] * 3,
        out_specs=anywhere,
        scratch_shapes=[
            pltpu.VMEM(grad.shape, jnp.float32),
            pltpu.VMEM(resid.shape, jnp.bfloat16),
            pltpu.VMEM(disp.shape, jnp.bfloat16),
            pltpu.VMEM(grad.shape, jnp.float32),
            pltpu.SemaphoreType.DMA((2 * tiles + 1,)),
            pltpu.SemaphoreType.DMA((tiles,)),
        ],
        compiler_params=pltpu.CompilerParams(vmem_limit_bytes=60 << 20),
    )(grad, resid, disp)


def local(eigvec, force_const, amplitudes, mlip_forces, frequency):
    return add_last(*exchange(eigvec.T, force_const, amplitudes, mlip_forces, frequency))


def solution(mesh):
    return jax.shard_map(
        local,
        mesh=mesh,
        in_specs=(
            P("row", ("col", "cfg")),
            P(("col", "cfg"), "row"),
            P(("col", "cfg"), None),
            P(("col", "cfg"), "row"),
            P(("col", "cfg")),
        ),
        out_specs=P(("col", "cfg"), "row"),
        check_vma=False,
    )
```

```python
import functools

import jax
import jax.numpy as jnp
from jax import lax
from jax.experimental import pallas as pl
from jax.experimental.pallas import tpu as pltpu
from jax.sharding import PartitionSpec as P

MESH = pl.DeviceIdType.MESH
PAIRS = 4
LANES = 128
TILE = 256
ORDER = [
    (0, 0), (0, 1), (1, 0, 1), (1, 0, 0), (0, 3), (1, 1, 0), (1, 1, 1), (2, 0, 0),
    (2, 0, 1), (0, 2), (2, 1, 0), (2, 1, 1), (3, 0, 1), (3, 0, 0), (1, 2, 0), (1, 2, 1),
    (1, 3, 1), (4, 0, 1), (1, 3, 0), (4, 0, 0), (3, 1, 1), (3, 1, 0), (2, 2, 0), (2, 2, 1),
    (5, 0, 1), (4, 1, 1), (5, 0, 0), (4, 1, 0), (2, 3, 1), (3, 2, 1), (2, 3, 0), (6, 0, 1),
    (3, 2, 0), (5, 1, 1), (6, 0, 0), (5, 1, 0), (4, 2, 1), (3, 3, 0), (3, 3, 1), (4, 2, 0),
    (7, 0), (6, 1, 0), (6, 1, 1), (4, 3, 1), (4, 3, 0), (5, 2, 0), (5, 2, 1), (8, 0),
    (7, 1), (6, 2, 0), (6, 2, 1), (5, 3, 0), (8, 1), (5, 3, 1), (9, 0, 0), (7, 2),
    (6, 3, 0), (6, 3, 1), (9, 0, 1), (9, 1, 0), (9, 1, 1), (8, 2), (7, 3), (10, 0),
    (8, 3), (11, 0), (10, 1), (12, 0, 0), (9, 2, 0), (12, 0, 1), (9, 2, 1), (11, 1),
    (12, 1, 0), (9, 3, 0), (9, 3, 1), (12, 0, 2), (12, 1, 1), (10, 2), (12, 1, 2), (11, 2),
    (12, 2, 0), (10, 3), (12, 2, 1), (12, 2, 2), (11, 3),
]


def comm_kernel(
    eig_hbm, fc_hbm, amp_hbm, forces_hbm, freq_hbm, grad_hbm, resid_hbm, disp_hbm,
    freq, eig_t, eig, fc, amp, scale, part32, part16, in_opp, in_near, sum32, sum16, in_second, own32, own16, in_zl,
    disp, harm, in_core, harm32, harm16, in_zh, force_in, force_own, resid, grad,
    load_sem, col_send, col_recv, row_send, row_recv, m_send, m_recv, out_sem,
):
    modes, rows = eig_hbm.shape
    quarter, sub = rows // 4, rows // 16
    half = quarter // 2
    out_rows = fc_hbm.shape[0]
    piece = out_rows // 4

    row, x, cfg = lax.axis_index("row"), lax.axis_index("col"), lax.axis_index("cfg")
    zh, core, y, zl = row // 2, row % 2, cfg // 2, cfg % 2

    def x_dev(d):
        return {"col": (x + d) % 4}

    def y_dev(d):
        return {"cfg": ((y + d) % 4) * 2 + zl}

    def zh_dev(d):
        return {"row": ((zh + d) % 4) * 2 + core}

    zl_dev = {"cfg": y * 2 + (1 - zl)}
    core_dev = {"row": zh * 2 + (1 - core)}
    axes = [(x, x_dev, y, y_dev), (y, y_dev, x, x_dev)]

    load_amp = [pltpu.make_async_copy(amp_hbm.at[:, pl.ds(p * 2 * LANES, 2 * LANES)], amp.at[p], load_sem.at[p]) for p in range(PAIRS)]
    load_eig = [pltpu.make_async_copy(eig_hbm.at[:, pl.ds(q * TILE, TILE)], eig_t.at[q], load_sem.at[13 + q]) for q in range(rows // TILE)]
    load_fc = pltpu.make_async_copy(fc_hbm, fc, load_sem.at[8])
    load_forces = [pltpu.make_async_copy(forces_hbm.at[pl.ds(q * piece, piece)], force_own.at[q], load_sem.at[9 + q]) for q in range(4)]
    load_freq = pltpu.make_async_copy(freq_hbm, freq, load_sem.at[13 + rows // TILE])
    for c in [load_freq] + load_amp[:1] + load_eig:
        c.start()

    barrier = pltpu.get_barrier_semaphore()
    peers = [x_dev(1), x_dev(2), x_dev(3), y_dev(1), y_dev(2), y_dev(3), zh_dev(1), zh_dev(2), zh_dev(3), zl_dev, core_dev]
    for dev in peers:
        pl.semaphore_signal(barrier, inc=1, device_id=dev, device_id_type=MESH)

    load_freq.wait()
    f = freq[...].reshape(1, modes)
    on_diag = lax.broadcasted_iota(jnp.int32, (modes, modes), 0) == lax.broadcasted_iota(jnp.int32, (modes, modes), 1)
    f_col = jnp.sum(jnp.where(on_diag, f, 0.0), axis=1, keepdims=True)
    scale[...] = jnp.broadcast_to(1.0 / jnp.sqrt(2.0 * f_col), scale.shape)

    for q, c in enumerate(load_eig):
        c.wait()
        eig[pl.ds(q * TILE, TILE)] = eig_t[q].T
    for c in load_amp[1:] + load_forces + [load_fc]:
        c.start()
    load_amp[0].wait()

    def col_copy(p, t, k, src, dst, dev):
        return pltpu.make_async_remote_copy(
            src_ref=src, dst_ref=dst, send_sem=col_send.at[p, t, k], recv_sem=col_recv.at[p, t, k],
            device_id=dev, device_id_type=MESH,
        )

    def row_copy(p, k, src, dst, dev):
        return pltpu.make_async_remote_copy(
            src_ref=src, dst_ref=dst, send_sem=row_send.at[p, k], recv_sem=row_recv.at[p, k],
            device_id=dev, device_id_type=MESH,
        )

    lo, hi = pl.ds(0, half), pl.ds(half, half)

    def first_out(p, t, k):
        a, a_dev, _, _ = axes[t]
        q1, q2, q3 = (a + 1) % 4, (a + 2) % 4, (a + 3) % 4
        src, dst, dev = [
            (part16.at[p, t, q2, lo], in_opp.at[p, t, 0], 1),
            (part16.at[p, t, q2, hi], in_opp.at[p, t, 1], 3),
            (part16.at[p, t, q1, hi], in_near.at[p, t, 0, hi], 1),
            (part16.at[p, t, q3, lo], in_near.at[p, t, 1, lo], 3),
            (part16.at[p, t, q1, lo], in_near.at[p, t, 0, lo], 1),
            (part16.at[p, t, q3, hi], in_near.at[p, t, 1, hi], 3),
        ][k]
        return col_copy(p, t, k, src, dst, a_dev(dev))

    def second_out(p, t, d):
        _, _, b, b_dev = axes[t]
        return col_copy(p, t, 5 + d, sum16.at[p, t, (b + d) % 4], in_second.at[p, t, d - 1], b_dev(d))

    def zl_out(p, t):
        return col_copy(p, t, 9, own16.at[p, t], in_zl.at[p, t], zl_dev)

    def disp_at(p, t, start, size, align):
        return disp.at[p, t, pl.ds(pl.multiple_of(start, align), size)]

    def spread_b(p, t, d, owner):
        a, _, _, b_dev = axes[t]
        at = disp_at(p, t, a * quarter + owner * sub, sub, 16)
        return col_copy(p, t, 9 + d, at, at, b_dev(d))

    def spread_a(p, t, k, owner):
        _, a_dev, _, _ = axes[t]
        which, dev = [(0, 1), (1, 1), (1, 3), (0, 3), (0, 1), (1, 3)][k]
        at = disp_at(p, t, owner * quarter + which * half, half, 16)
        return col_copy(p, t, 13 + k, at, at, a_dev(dev))

    def core_out(p):
        return row_copy(p, 0, harm.at[p, 1 - core], in_core.at[p], core_dev)

    cut = piece // 32 * 16
    portions = [(0, piece - cut), (piece - cut, cut)]

    def zh_out(p, d, h):
        at = pl.ds(*portions[h])
        return row_copy(p, 2 * d - 1 + h, harm16.at[p, (zh + d) % 4, at], in_zh.at[p, d - 1, at], zh_dev(d))

    def resid_rows(owner, h):
        start, size = portions[h]
        return pl.ds(pl.multiple_of(owner * piece + start, 16), size)

    def resid_spread(p, d, h, owner):
        at = resid.at[p, core, resid_rows(owner, h)]
        return row_copy(p, 2 * d + 5 + h, at, at, zh_dev(d))

    def resid_core(p, which):
        at = resid.at[p, which]
        return row_copy(p, 13, at, at, core_dev)

    def disp_store(t):
        return pltpu.make_async_copy(disp.at[PAIRS - 1, t], disp_hbm.at[:, pl.ds(t * LANES, LANES)], out_sem.at[t])

    def resid_store(t):
        return pltpu.make_async_copy(resid.at[PAIRS - 1, t], resid_hbm.at[:, pl.ds(t * LANES, LANES)], out_sem.at[2 + t])

    def grad_store(g):
        at = pl.ds(g * 3 * TILE, 3 * TILE)
        return pltpu.make_async_copy(grad.at[:, at], grad_hbm.at[:, at], out_sem.at[4 + g])

    def force_out(d, slot):
        return pltpu.make_async_remote_copy(
            src_ref=force_own.at[(zh + d) % 4], dst_ref=force_in.at[slot],
            send_sem=m_send.at[d - 1], recv_sem=m_recv.at[d - 1], device_id=zh_dev(d), device_id_type=MESH,
        )

    def first_part():
        scaled = (scale[:, :1] * amp[0].astype(jnp.float32)).astype(jnp.bfloat16)

        def one(t, d):
            q = (axes[t][0] + d) % 4
            block = jnp.dot(
                eig[pl.ds(pl.multiple_of(q * quarter, 16), quarter)],
                scaled[:, t * LANES : (t + 1) * LANES],
                preferred_element_type=jnp.float32,
            )
            part32[0, t, q] = block
            part16[0, t, q] = block.astype(jnp.bfloat16)

        for t in range(2):
            one(t, 2)
        pl.semaphore_wait(barrier, len(peers))
        for k in range(2):
            for t in range(2):
                first_out(0, t, k).start()
        for d, k in ((1, 2), (3, 3)):
            for t in range(2):
                one(t, d)
                first_out(0, t, k).start()
        for t in range(2):
            one(t, 0)

    def compute_part(p):
        load_amp[p].wait()
        scaled = (scale[:, :1] * amp[p].astype(jnp.float32)).astype(jnp.bfloat16)

        def one(q, carry):
            product = jnp.dot(eig[pl.ds(pl.multiple_of(q * quarter, 16), quarter)], scaled, preferred_element_type=jnp.float32)
            for t in range(2):
                block = product[:, t * LANES : (t + 1) * LANES]
                part32[p, t, q] = block
                part16[p, t, q] = block.astype(jnp.bfloat16)
            return carry

        lax.fori_loop(0, 4, one, 0)

    def send_part(p):
        for k in range(4):
            for t in range(2):
                first_out(p, t, k).start()

    harm_first = [step[1] for step in ORDER if step[0] == 7][0]
    grad_pairs = [[step[1] for step in ORDER if step[0] == 12 and step[2] == g] for g in range(3)]

    def stage0(p):
        if p == 0:
            first_part()
            for c in load_forces:
                c.wait()
            force_in[zh] = force_own[zh]
            for d in (1, 2, 3):
                force_out(d, zh).start()
        else:
            compute_part(p)
            send_part(p)

    def stage1(p, t):
        a = axes[t][0]
        first_out(p, t, 0).wait_recv()
        q1, q3 = (a + 1) % 4, (a + 3) % 4
        part16[p, t, q1, lo] = (part32[p, t, q1, lo] + in_opp[p, t, 0].astype(jnp.float32)).astype(jnp.bfloat16)
        first_out(p, t, 4).start()
        first_out(p, t, 1).wait_recv()
        part16[p, t, q3, hi] = (part32[p, t, q3, hi] + in_opp[p, t, 1].astype(jnp.float32)).astype(jnp.bfloat16)
        first_out(p, t, 5).start()

    def stage2(p, t):
        a, _, b, _ = axes[t]
        for k in range(2, 6):
            first_out(p, t, k).wait_recv()
        total = part32[p, t, a] + in_near[p, t, 0].astype(jnp.float32) + in_near[p, t, 1].astype(jnp.float32)
        total = total.reshape(4, sub, LANES)
        sum32[p, t] = total
        sum16[p, t] = total.astype(jnp.bfloat16)
        for d in (2, 1, 3):
            second_out(p, t, d).start()

    def stage3(p, t):
        b = axes[t][2]
        for d in (1, 2, 3):
            second_out(p, t, d).wait_recv()
        total = sum32[p, t, b]
        for d in range(3):
            total += in_second[p, t, d].astype(jnp.float32)
        own32[p, t] = total
        own16[p, t] = total.astype(jnp.bfloat16)
        zl_out(p, t).start()

    def stage4(p, t):
        a, _, b, _ = axes[t]
        zl_out(p, t).wait_recv()
        value = (own32[p, t] + in_zl[p, t].astype(jnp.float32)).astype(jnp.bfloat16)
        disp[p, t, pl.ds(pl.multiple_of(a * quarter + b * sub, 16), sub)] = value
        for d in (2, 1, 3):
            spread_b(p, t, d, b).start()

    def stage5(p, t):
        a, _, b, _ = axes[t]
        for d in (1, 2, 3):
            spread_b(p, t, d, (b + 4 - d) % 4).wait_recv()
        for k in (0, 2, 1, 3):
            spread_a(p, t, k, a).start()

    def stage6(p, t):
        a = axes[t][0]
        below, above = (a + 3) % 4, (a + 1) % 4
        spread_a(p, t, 0, below).wait_recv()
        spread_a(p, t, 4, below).start()
        spread_a(p, t, 2, above).wait_recv()
        spread_a(p, t, 5, above).start()

    def stage7(p):
        for t in range(2):
            a = axes[t][0]
            below, above, far = (a + 3) % 4, (a + 1) % 4, (a + 2) % 4
            spread_a(p, t, 1, below).wait_recv()
            spread_a(p, t, 3, above).wait_recv()
            spread_a(p, t, 4, far).wait_recv()
            spread_a(p, t, 5, far).wait_recv()
        if p == PAIRS - 1:
            for t in range(2):
                disp_store(t).start()
        if p == harm_first:
            load_fc.wait()
            for d in (1, 2, 3):
                force_out(d, (zh + 4 - d) % 4).wait_recv()

        product = jnp.dot(fc[...], jnp.concatenate([disp[p, 0], disp[p, 1]], axis=1), preferred_element_type=jnp.float32)
        for t in range(2):
            harm[p, t] = product[:, t * LANES : (t + 1) * LANES]
        core_out(p).start()

    def stage8(p):
        core_out(p).wait_recv()
        total = (harm[p, core] + in_core[p]).reshape(4, piece, LANES)
        harm32[p] = total
        harm16[p] = total.astype(jnp.bfloat16)
        for h in range(2):
            for d in (2, 1, 3):
                zh_out(p, d, h).start()

    def stage9(p, h):
        for d in (1, 2, 3):
            zh_out(p, d, h).wait_recv()
        at = pl.ds(*portions[h])
        total = force_in[p, at].astype(jnp.float32) + harm32[p, zh, at]
        for d in range(3):
            total += in_zh[p, d, at].astype(jnp.float32)
        resid[p, core, resid_rows(zh, h)] = total.astype(jnp.bfloat16)
        for d in (2, 1, 3):
            resid_spread(p, d, h, zh).start()

    def stage10(p):
        for h in range(2):
            for d in (1, 2, 3):
                resid_spread(p, d, h, (zh + 4 - d) % 4).wait_recv()
        resid_core(p, core).start()

    def stage11(p):
        resid_core(p, 1 - core).wait_recv()
        if p == PAIRS - 1:
            for t in range(2):
                resid_store(t).start()

    def stage12(p, g):
        left = jnp.concatenate([resid[p, 0], resid[p, 1]], axis=1)
        for c in range(g * 3, g * 3 + 3):
            at = pl.ds(c * TILE, TILE)
            right = jnp.concatenate([disp[p, 0, at], disp[p, 1, at]], axis=1)
            term = lax.dot_general(left, right, (((1,), (1,)), ((), ())), preferred_element_type=jnp.float32)
            if p != grad_pairs[g][0]:
                term += grad[:, at]
            grad[:, at] = term
        if p == grad_pairs[g][-1]:
            grad_store(g).start()

    stages = [stage0, stage1, stage2, stage3, stage4, stage5, stage6, stage7, stage8, stage9, stage10, stage11, stage12]
    for s, *which in ORDER:
        stages[s](*which)

    def drain(p, carry):
        for t in range(2):
            a, _, b, _ = axes[t]
            for k in range(6):
                first_out(p, t, k).wait_send()
                spread_a(p, t, k, a).wait_send()
            for d in (1, 2, 3):
                second_out(p, t, d).wait_send()
                spread_b(p, t, d, b).wait_send()
            zl_out(p, t).wait_send()
        core_out(p).wait_send()
        for h in range(2):
            for d in (1, 2, 3):
                zh_out(p, d, h).wait_send()
                resid_spread(p, d, h, zh).wait_send()
        resid_core(p, core).wait_send()
        return carry

    lax.fori_loop(0, PAIRS, drain, 0)
    for t in range(2):
        disp_store(t).wait()
        resid_store(t).wait()
    for g in range(3):
        grad_store(g).wait()
    for d in (1, 2, 3):
        force_out(d, zh).wait_send()


def exchange(eigvec, force_const, amplitudes, mlip_forces, frequency):
    modes, rows = eigvec.shape
    out_rows = force_const.shape[0]
    quarter, sub, piece = rows // 4, rows // 16, out_rows // 4
    half = quarter // 2
    bf16, f32 = jnp.bfloat16, jnp.float32
    anywhere = pl.BlockSpec(memory_space=pl.ANY)
    dma = pltpu.SemaphoreType.DMA
    return pl.pallas_call(
        comm_kernel,
        name="exchange",
        out_shape=[
            jax.ShapeDtypeStruct((out_rows, rows), f32),
            jax.ShapeDtypeStruct((out_rows, 2 * LANES), bf16),
            jax.ShapeDtypeStruct((rows, 2 * LANES), bf16),
        ],
        in_specs=[anywhere] * 5,
        out_specs=[anywhere] * 3,
        scratch_shapes=[
            pltpu.VMEM((modes,), f32),
            pltpu.VMEM((rows // TILE, modes, TILE), bf16),
            pltpu.VMEM((rows, modes), bf16),
            pltpu.VMEM((out_rows, rows), bf16),
            pltpu.VMEM((PAIRS, modes, 2 * LANES), bf16),
            pltpu.VMEM((modes, LANES), f32),
            pltpu.VMEM((PAIRS, 2, 4, quarter, LANES), f32),
            pltpu.VMEM((PAIRS, 2, 4, quarter, LANES), bf16),
            pltpu.VMEM((PAIRS, 2, 2, half, LANES), bf16),
            pltpu.VMEM((PAIRS, 2, 2, quarter, LANES), bf16),
            pltpu.VMEM((PAIRS, 2, 4, sub, LANES), f32),
            pltpu.VMEM((PAIRS, 2, 4, sub, LANES), bf16),
            pltpu.VMEM((PAIRS, 2, 3, sub, LANES), bf16),
            pltpu.VMEM((PAIRS, 2, sub, LANES), f32),
            pltpu.VMEM((PAIRS, 2, sub, LANES), bf16),
            pltpu.VMEM((PAIRS, 2, sub, LANES), bf16),
            pltpu.VMEM((PAIRS, 2, rows, LANES), bf16),
            pltpu.VMEM((PAIRS, 2, out_rows, LANES), f32),
            pltpu.VMEM((PAIRS, out_rows, LANES), f32),
            pltpu.VMEM((PAIRS, 4, piece, LANES), f32),
            pltpu.VMEM((PAIRS, 4, piece, LANES), bf16),
            pltpu.VMEM((PAIRS, 3, piece, LANES), bf16),
            pltpu.VMEM((PAIRS, piece, LANES), bf16),
            pltpu.VMEM((4, piece, LANES), bf16),
            pltpu.VMEM((PAIRS, 2, out_rows, LANES), bf16),
            pltpu.VMEM((out_rows, rows), f32),
            dma((14 + rows // TILE,)),
            dma((PAIRS, 2, 19)),
            dma((PAIRS, 2, 19)),
            dma((PAIRS, 14)),
            dma((PAIRS, 14)),
            dma((3,)),
            dma((3,)),
            dma((7,)),
        ],
        compiler_params=pltpu.CompilerParams(
            collective_id=0, has_side_effects=True, vmem_limit_bytes=60 << 20
        ),
    )(eigvec, force_const, amplitudes, mlip_forces, frequency)


def last_kernel(grad_hbm, resid_hbm, disp_hbm, out_hbm, grad, resid, disp, total, load_sem, store_sem):
    tiles = disp.shape[0] // TILE

    def load_grad(c):
        at = pl.ds(c * TILE, TILE)
        return pltpu.make_async_copy(grad_hbm.at[:, at], grad.at[:, at], load_sem.at[c])

    def store(c):
        at = pl.ds(c * TILE, TILE)
        return pltpu.make_async_copy(total.at[:, at], out_hbm.at[:, at], store_sem.at[c])

    load_resid = pltpu.make_async_copy(resid_hbm, resid, load_sem.at[tiles])

    def load_disp(c):
        at = pl.ds(c * TILE, TILE)
        return pltpu.make_async_copy(disp_hbm.at[at], disp.at[at], load_sem.at[tiles + 1 + c])

    load_resid.start()
    for c in range(tiles):
        load_disp(c).start()
        load_grad(c).start()
    load_resid.wait()
    for c in range(tiles):
        at = pl.ds(c * TILE, TILE)
        load_disp(c).wait()
        term = lax.dot_general(resid[...], disp[at], (((1,), (1,)), ((), ())), preferred_element_type=jnp.float32)
        load_grad(c).wait()
        total[:, at] = (grad[:, at] + term) * (1.0 / 32.0)
        store(c).start()
    for c in range(tiles):
        store(c).wait()


def add_last(grad, resid, disp):
    anywhere = pl.BlockSpec(memory_space=pl.ANY)
    tiles = disp.shape[0] // TILE
    return pl.pallas_call(
        last_kernel,
        name="add_last",
        out_shape=jax.ShapeDtypeStruct(grad.shape, jnp.float32),
        in_specs=[anywhere] * 3,
        out_specs=anywhere,
        scratch_shapes=[
            pltpu.VMEM(grad.shape, jnp.float32),
            pltpu.VMEM(resid.shape, jnp.bfloat16),
            pltpu.VMEM(disp.shape, jnp.bfloat16),
            pltpu.VMEM(grad.shape, jnp.float32),
            pltpu.SemaphoreType.DMA((2 * tiles + 1,)),
            pltpu.SemaphoreType.DMA((tiles,)),
        ],
        compiler_params=pltpu.CompilerParams(vmem_limit_bytes=60 << 20),
    )(grad, resid, disp)


def local(eigvec, force_const, amplitudes, mlip_forces, frequency):
    return add_last(*exchange(eigvec.T, force_const, amplitudes, mlip_forces, frequency))


def solution(mesh):
    return jax.shard_map(
        local,
        mesh=mesh,
        in_specs=(
            P("row", ("col", "cfg")),
            P(("col", "cfg"), "row"),
            P(("col", "cfg"), None),
            P(("col", "cfg"), "row"),
            P(("col", "cfg")),
        ),
        out_specs=P(("col", "cfg"), "row"),
        check_vma=False,
    )
```

```python
import functools

import jax
import jax.numpy as jnp
from jax import lax
from jax.experimental import pallas as pl
from jax.experimental.pallas import tpu as pltpu
from jax.sharding import PartitionSpec as P

MESH = pl.DeviceIdType.MESH
PAIRS = 4
LANES = 128
TILE = 256
ORDER = [
    (0, 0), (0, 1), (1, 0, 1), (1, 0, 0), (0, 3), (1, 1, 0), (1, 1, 1), (2, 0, 0),
    (2, 0, 1), (0, 2), (2, 1, 0), (2, 1, 1), (3, 0, 1), (3, 0, 0), (1, 2, 0), (1, 2, 1),
    (1, 3, 1), (4, 0, 1), (1, 3, 0), (4, 0, 0), (3, 1, 1), (3, 1, 0), (2, 2, 0), (2, 2, 1),
    (5, 0, 1), (4, 1, 1), (5, 0, 0), (4, 1, 0), (2, 3, 1), (3, 2, 1), (2, 3, 0), (6, 0, 1),
    (3, 2, 0), (5, 1, 1), (6, 0, 0), (5, 1, 0), (4, 2, 1), (3, 3, 0), (3, 3, 1), (4, 2, 0),
    (7, 0), (6, 1, 0), (6, 1, 1), (4, 3, 1), (4, 3, 0), (5, 2, 0), (5, 2, 1), (8, 0),
    (7, 1), (6, 2, 0), (6, 2, 1), (5, 3, 0), (8, 1), (5, 3, 1), (9, 0, 0), (7, 2),
    (6, 3, 0), (6, 3, 1), (9, 0, 1), (9, 1, 0), (9, 1, 1), (8, 2), (7, 3), (10, 0),
    (8, 3), (11, 0), (10, 1), (12, 0, 0), (9, 2, 0), (12, 0, 1), (9, 2, 1), (11, 1),
    (12, 1, 0), (9, 3, 0), (9, 3, 1), (12, 0, 2), (12, 1, 1), (10, 2), (12, 1, 2), (11, 2),
    (12, 2, 0), (10, 3), (12, 2, 1), (12, 2, 2), (11, 3),
]


def comm_kernel(
    eig_hbm, fc_hbm, amp_hbm, forces_hbm, freq_hbm, grad_hbm, resid_hbm, disp_hbm,
    freq, eig_t, eig, fc, amp, scale, part32, part16, in_opp, in_near, sum32, sum16, in_second, own32, own16, in_zl,
    disp, harm, in_core, harm32, harm16, in_zh, force_in, force_own, resid, grad,
    load_sem, col_send, col_recv, row_send, row_recv, m_send, m_recv, out_sem,
):
    modes, rows = eig_hbm.shape
    quarter, sub = rows // 4, rows // 16
    half = quarter // 2
    out_rows = fc_hbm.shape[0]
    piece = out_rows // 4

    row, x, cfg = lax.axis_index("row"), lax.axis_index("col"), lax.axis_index("cfg")
    zh, core, y, zl = row // 2, row % 2, cfg // 2, cfg % 2

    def x_dev(d):
        return {"col": (x + d) % 4}

    def y_dev(d):
        return {"cfg": ((y + d) % 4) * 2 + zl}

    def zh_dev(d):
        return {"row": ((zh + d) % 4) * 2 + core}

    zl_dev = {"cfg": y * 2 + (1 - zl)}
    core_dev = {"row": zh * 2 + (1 - core)}
    axes = [(x, x_dev, y, y_dev), (y, y_dev, x, x_dev)]

    load_amp = [pltpu.make_async_copy(amp_hbm.at[:, pl.ds(p * 2 * LANES, 2 * LANES)], amp.at[p], load_sem.at[p]) for p in range(PAIRS)]
    load_eig = [pltpu.make_async_copy(eig_hbm.at[:, pl.ds(q * TILE, TILE)], eig_t.at[q], load_sem.at[13 + q]) for q in range(rows // TILE)]
    load_fc = pltpu.make_async_copy(fc_hbm, fc, load_sem.at[8])
    load_forces = [pltpu.make_async_copy(forces_hbm.at[pl.ds(q * piece, piece)], force_own.at[q], load_sem.at[9 + q]) for q in range(4)]
    load_freq = pltpu.make_async_copy(freq_hbm, freq, load_sem.at[13 + rows // TILE])
    for c in [load_freq] + load_amp[:1] + load_eig:
        c.start()

    barrier = pltpu.get_barrier_semaphore()
    peers = [x_dev(1), x_dev(2), x_dev(3), y_dev(1), y_dev(2), y_dev(3), zh_dev(1), zh_dev(2), zh_dev(3), zl_dev, core_dev]
    for dev in peers:
        pl.semaphore_signal(barrier, inc=1, device_id=dev, device_id_type=MESH)

    load_freq.wait()
    f = freq[...].reshape(1, modes)
    on_diag = lax.broadcasted_iota(jnp.int32, (modes, modes), 0) == lax.broadcasted_iota(jnp.int32, (modes, modes), 1)
    f_col = jnp.sum(jnp.where(on_diag, f, 0.0), axis=1, keepdims=True)
    scale[...] = jnp.broadcast_to(1.0 / jnp.sqrt(2.0 * f_col), scale.shape)

    for q, c in enumerate(load_eig):
        c.wait()
        eig[pl.ds(q * TILE, TILE)] = eig_t[q].T
    for c in load_amp[1:] + load_forces + [load_fc]:
        c.start()
    load_amp[0].wait()

    def col_copy(p, t, k, src, dst, dev):
        return pltpu.make_async_remote_copy(
            src_ref=src, dst_ref=dst, send_sem=col_send.at[p, t, k], recv_sem=col_recv.at[p, t, k],
            device_id=dev, device_id_type=MESH,
        )

    def row_copy(p, k, src, dst, dev):
        return pltpu.make_async_remote_copy(
            src_ref=src, dst_ref=dst, send_sem=row_send.at[p, k], recv_sem=row_recv.at[p, k],
            device_id=dev, device_id_type=MESH,
        )

    lo, hi = pl.ds(0, half), pl.ds(half, half)

    def first_out(p, t, k):
        a, a_dev, _, _ = axes[t]
        q1, q2, q3 = (a + 1) % 4, (a + 2) % 4, (a + 3) % 4
        src, dst, dev = [
            (part16.at[p, t, q2, lo], in_opp.at[p, t, 0], 1),
            (part16.at[p, t, q2, hi], in_opp.at[p, t, 1], 3),
            (part16.at[p, t, q1, hi], in_near.at[p, t, 0, hi], 1),
            (part16.at[p, t, q3, lo], in_near.at[p, t, 1, lo], 3),
            (part16.at[p, t, q1, lo], in_near.at[p, t, 0, lo], 1),
            (part16.at[p, t, q3, hi], in_near.at[p, t, 1, hi], 3),
        ][k]
        return col_copy(p, t, k, src, dst, a_dev(dev))

    def second_out(p, t, d):
        _, _, b, b_dev = axes[t]
        return col_copy(p, t, 5 + d, sum16.at[p, t, (b + d) % 4], in_second.at[p, t, d - 1], b_dev(d))

    def zl_out(p, t):
        return col_copy(p, t, 9, own16.at[p, t], in_zl.at[p, t], zl_dev)

    def disp_at(p, t, start, size, align):
        return disp.at[p, t, pl.ds(pl.multiple_of(start, align), size)]

    def spread_b(p, t, d, owner):
        a, _, _, b_dev = axes[t]
        at = disp_at(p, t, a * quarter + owner * sub, sub, 16)
        return col_copy(p, t, 9 + d, at, at, b_dev(d))

    def spread_a(p, t, k, owner):
        _, a_dev, _, _ = axes[t]
        which, dev = [(0, 1), (1, 1), (1, 3), (0, 3), (0, 1), (1, 3)][k]
        at = disp_at(p, t, owner * quarter + which * half, half, 16)
        return col_copy(p, t, 13 + k, at, at, a_dev(dev))

    def core_out(p):
        return row_copy(p, 0, harm.at[p, 1 - core], in_core.at[p], core_dev)

    cut = piece // 32 * 16
    portions = [(0, piece - cut), (piece - cut, cut)]

    def zh_out(p, d, h):
        at = pl.ds(*portions[h])
        return row_copy(p, 2 * d - 1 + h, harm16.at[p, (zh + d) % 4, at], in_zh.at[p, d - 1, at], zh_dev(d))

    def resid_rows(owner, h):
        start, size = portions[h]
        return pl.ds(pl.multiple_of(owner * piece + start, 16), size)

    def resid_spread(p, d, h, owner):
        at = resid.at[p, core, resid_rows(owner, h)]
        return row_copy(p, 2 * d + 5 + h, at, at, zh_dev(d))

    def resid_core(p, which):
        at = resid.at[p, which]
        return row_copy(p, 13, at, at, core_dev)

    def disp_store(t):
        return pltpu.make_async_copy(disp.at[PAIRS - 1, t], disp_hbm.at[:, pl.ds(t * LANES, LANES)], out_sem.at[t])

    def resid_store(t):
        return pltpu.make_async_copy(resid.at[PAIRS - 1, t], resid_hbm.at[:, pl.ds(t * LANES, LANES)], out_sem.at[2 + t])

    def grad_store(g):
        at = pl.ds(g * 3 * TILE, 3 * TILE)
        return pltpu.make_async_copy(grad.at[:, at], grad_hbm.at[:, at], out_sem.at[4 + g])

    def force_out(d, slot):
        return pltpu.make_async_remote_copy(
            src_ref=force_own.at[(zh + d) % 4], dst_ref=force_in.at[slot],
            send_sem=m_send.at[d - 1], recv_sem=m_recv.at[d - 1], device_id=zh_dev(d), device_id_type=MESH,
        )

    def first_part():
        scaled = (scale[:, :1] * amp[0].astype(jnp.float32)).astype(jnp.bfloat16)

        def one(t, d):
            q = (axes[t][0] + d) % 4
            block = jnp.dot(
                eig[pl.ds(pl.multiple_of(q * quarter, 16), quarter)],
                scaled[:, t * LANES : (t + 1) * LANES],
                preferred_element_type=jnp.float32,
            )
            part32[0, t, q] = block
            part16[0, t, q] = block.astype(jnp.bfloat16)

        for t in range(2):
            one(t, 2)
        pl.semaphore_wait(barrier, len(peers))
        for k in range(2):
            for t in range(2):
                first_out(0, t, k).start()
        for d, k in ((1, 2), (3, 3)):
            for t in range(2):
                one(t, d)
                first_out(0, t, k).start()
        for t in range(2):
            one(t, 0)

    def compute_part(p):
        load_amp[p].wait()
        scaled = (scale[:, :1] * amp[p].astype(jnp.float32)).astype(jnp.bfloat16)

        def one(q, carry):
            product = jnp.dot(eig[pl.ds(pl.multiple_of(q * quarter, 16), quarter)], scaled, preferred_element_type=jnp.float32)
            for t in range(2):
                block = product[:, t * LANES : (t + 1) * LANES]
                part32[p, t, q] = block
                part16[p, t, q] = block.astype(jnp.bfloat16)
            return carry

        lax.fori_loop(0, 4, one, 0)

    def send_part(p):
        for k in range(4):
            for t in range(2):
                first_out(p, t, k).start()

    harm_first = [step[1] for step in ORDER if step[0] == 7][0]
    grad_pairs = [[step[1] for step in ORDER if step[0] == 12 and step[2] == g] for g in range(3)]

    def stage0(p):
        if p == 0:
            first_part()
            for c in load_forces:
                c.wait()
            force_in[zh] = force_own[zh]
            for d in (1, 2, 3):
                force_out(d, zh).start()
        else:
            compute_part(p)
            send_part(p)

    def stage1(p, t):
        a = axes[t][0]
        first_out(p, t, 0).wait_recv()
        q1, q3 = (a + 1) % 4, (a + 3) % 4
        part16[p, t, q1, lo] = (part32[p, t, q1, lo] + in_opp[p, t, 0].astype(jnp.float32)).astype(jnp.bfloat16)
        first_out(p, t, 4).start()
        first_out(p, t, 1).wait_recv()
        part16[p, t, q3, hi] = (part32[p, t, q3, hi] + in_opp[p, t, 1].astype(jnp.float32)).astype(jnp.bfloat16)
        first_out(p, t, 5).start()

    def stage2(p, t):
        a, _, b, _ = axes[t]
        for k in range(2, 6):
            first_out(p, t, k).wait_recv()
        total = part32[p, t, a] + in_near[p, t, 0].astype(jnp.float32) + in_near[p, t, 1].astype(jnp.float32)
        total = total.reshape(4, sub, LANES)
        sum32[p, t] = total
        sum16[p, t] = total.astype(jnp.bfloat16)
        for d in (2, 1, 3):
            second_out(p, t, d).start()

    def stage3(p, t):
        b = axes[t][2]
        for d in (1, 2, 3):
            second_out(p, t, d).wait_recv()
        total = sum32[p, t, b]
        for d in range(3):
            total += in_second[p, t, d].astype(jnp.float32)
        own32[p, t] = total
        own16[p, t] = total.astype(jnp.bfloat16)
        zl_out(p, t).start()

    def stage4(p, t):
        a, _, b, _ = axes[t]
        zl_out(p, t).wait_recv()
        value = (own32[p, t] + in_zl[p, t].astype(jnp.float32)).astype(jnp.bfloat16)
        disp[p, t, pl.ds(pl.multiple_of(a * quarter + b * sub, 16), sub)] = value
        for d in (2, 1, 3):
            spread_b(p, t, d, b).start()

    def stage5(p, t):
        a, _, b, _ = axes[t]
        for d in (1, 2, 3):
            spread_b(p, t, d, (b + 4 - d) % 4).wait_recv()
        for k in (0, 2, 1, 3):
            spread_a(p, t, k, a).start()

    def stage6(p, t):
        a = axes[t][0]
        below, above = (a + 3) % 4, (a + 1) % 4
        spread_a(p, t, 0, below).wait_recv()
        spread_a(p, t, 4, below).start()
        spread_a(p, t, 2, above).wait_recv()
        spread_a(p, t, 5, above).start()

    def stage7(p):
        for t in range(2):
            a = axes[t][0]
            below, above, far = (a + 3) % 4, (a + 1) % 4, (a + 2) % 4
            spread_a(p, t, 1, below).wait_recv()
            spread_a(p, t, 3, above).wait_recv()
            spread_a(p, t, 4, far).wait_recv()
            spread_a(p, t, 5, far).wait_recv()
        if p == PAIRS - 1:
            for t in range(2):
                disp_store(t).start()
        if p == harm_first:
            load_fc.wait()
            for d in (1, 2, 3):
                force_out(d, (zh + 4 - d) % 4).wait_recv()

        product = jnp.dot(fc[...], jnp.concatenate([disp[p, 0], disp[p, 1]], axis=1), preferred_element_type=jnp.float32)
        for t in range(2):
            harm[p, t] = product[:, t * LANES : (t + 1) * LANES]
        core_out(p).start()

    def stage8(p):
        core_out(p).wait_recv()
        total = (harm[p, core] + in_core[p]).reshape(4, piece, LANES)
        harm32[p] = total
        harm16[p] = total.astype(jnp.bfloat16)
        for h in range(2):
            for d in (2, 1, 3):
                zh_out(p, d, h).start()

    def stage9(p, h):
        for d in (1, 2, 3):
            zh_out(p, d, h).wait_recv()
        at = pl.ds(*portions[h])
        total = force_in[p, at].astype(jnp.float32) + harm32[p, zh, at]
        for d in range(3):
            total += in_zh[p, d, at].astype(jnp.float32)
        resid[p, core, resid_rows(zh, h)] = total.astype(jnp.bfloat16)
        for d in (2, 1, 3):
            resid_spread(p, d, h, zh).start()

    def stage10(p):
        for h in range(2):
            for d in (1, 2, 3):
                resid_spread(p, d, h, (zh + 4 - d) % 4).wait_recv()
        resid_core(p, core).start()

    def stage11(p):
        resid_core(p, 1 - core).wait_recv()
        if p == PAIRS - 1:
            for t in range(2):
                resid_store(t).start()

    def stage12(p, g):
        left = jnp.concatenate([resid[p, 0], resid[p, 1]], axis=1)
        for c in range(g * 3, g * 3 + 3):
            at = pl.ds(c * TILE, TILE)
            right = jnp.concatenate([disp[p, 0, at], disp[p, 1, at]], axis=1)
            term = lax.dot_general(left, right, (((1,), (1,)), ((), ())), preferred_element_type=jnp.float32)
            if p != grad_pairs[g][0]:
                term += grad[:, at]
            grad[:, at] = term
        if p == grad_pairs[g][-1]:
            grad_store(g).start()

    stages = [stage0, stage1, stage2, stage3, stage4, stage5, stage6, stage7, stage8, stage9, stage10, stage11, stage12]

    def drain(p, carry):
        for t in range(2):
            a, _, b, _ = axes[t]
            for k in range(6):
                first_out(p, t, k).wait_send()
                spread_a(p, t, k, a).wait_send()
            for d in (1, 2, 3):
                second_out(p, t, d).wait_send()
                spread_b(p, t, d, b).wait_send()
            zl_out(p, t).wait_send()
        core_out(p).wait_send()
        for h in range(2):
            for d in (1, 2, 3):
                zh_out(p, d, h).wait_send()
        return carry

    def drain_resid(p, carry):
        for h in range(2):
            for d in (1, 2, 3):
                resid_spread(p, d, h, zh).wait_send()
        resid_core(p, core).wait_send()
        return carry

    quiet = max(i for i, step in enumerate(ORDER) if step[0] == 10)
    for i, (s, *which) in enumerate(ORDER):
        if i == quiet:
            lax.fori_loop(0, PAIRS, drain, 0)
        stages[s](*which)
    lax.fori_loop(0, PAIRS, drain_resid, 0)
    for t in range(2):
        disp_store(t).wait()
        resid_store(t).wait()
    for g in range(3):
        grad_store(g).wait()
    for d in (1, 2, 3):
        force_out(d, zh).wait_send()


def exchange(eigvec, force_const, amplitudes, mlip_forces, frequency):
    modes, rows = eigvec.shape
    out_rows = force_const.shape[0]
    quarter, sub, piece = rows // 4, rows // 16, out_rows // 4
    half = quarter // 2
    bf16, f32 = jnp.bfloat16, jnp.float32
    anywhere = pl.BlockSpec(memory_space=pl.ANY)
    dma = pltpu.SemaphoreType.DMA
    return pl.pallas_call(
        comm_kernel,
        name="exchange",
        out_shape=[
            jax.ShapeDtypeStruct((out_rows, rows), f32),
            jax.ShapeDtypeStruct((out_rows, 2 * LANES), bf16),
            jax.ShapeDtypeStruct((rows, 2 * LANES), bf16),
        ],
        in_specs=[anywhere] * 5,
        out_specs=[anywhere] * 3,
        scratch_shapes=[
            pltpu.VMEM((modes,), f32),
            pltpu.VMEM((rows // TILE, modes, TILE), bf16),
            pltpu.VMEM((rows, modes), bf16),
            pltpu.VMEM((out_rows, rows), bf16),
            pltpu.VMEM((PAIRS, modes, 2 * LANES), bf16),
            pltpu.VMEM((modes, LANES), f32),
            pltpu.VMEM((PAIRS, 2, 4, quarter, LANES), f32),
            pltpu.VMEM((PAIRS, 2, 4, quarter, LANES), bf16),
            pltpu.VMEM((PAIRS, 2, 2, half, LANES), bf16),
            pltpu.VMEM((PAIRS, 2, 2, quarter, LANES), bf16),
            pltpu.VMEM((PAIRS, 2, 4, sub, LANES), f32),
            pltpu.VMEM((PAIRS, 2, 4, sub, LANES), bf16),
            pltpu.VMEM((PAIRS, 2, 3, sub, LANES), bf16),
            pltpu.VMEM((PAIRS, 2, sub, LANES), f32),
            pltpu.VMEM((PAIRS, 2, sub, LANES), bf16),
            pltpu.VMEM((PAIRS, 2, sub, LANES), bf16),
            pltpu.VMEM((PAIRS, 2, rows, LANES), bf16),
            pltpu.VMEM((PAIRS, 2, out_rows, LANES), f32),
            pltpu.VMEM((PAIRS, out_rows, LANES), f32),
            pltpu.VMEM((PAIRS, 4, piece, LANES), f32),
            pltpu.VMEM((PAIRS, 4, piece, LANES), bf16),
            pltpu.VMEM((PAIRS, 3, piece, LANES), bf16),
            pltpu.VMEM((PAIRS, piece, LANES), bf16),
            pltpu.VMEM((4, piece, LANES), bf16),
            pltpu.VMEM((PAIRS, 2, out_rows, LANES), bf16),
            pltpu.VMEM((out_rows, rows), f32),
            dma((14 + rows // TILE,)),
            dma((PAIRS, 2, 19)),
            dma((PAIRS, 2, 19)),
            dma((PAIRS, 14)),
            dma((PAIRS, 14)),
            dma((3,)),
            dma((3,)),
            dma((7,)),
        ],
        compiler_params=pltpu.CompilerParams(
            collective_id=0, has_side_effects=True, vmem_limit_bytes=60 << 20
        ),
    )(eigvec, force_const, amplitudes, mlip_forces, frequency)


def last_kernel(grad_hbm, resid_hbm, disp_hbm, out_hbm, grad, resid, disp, total, load_sem, store_sem):
    tiles = disp.shape[0] // TILE

    def load_grad(c):
        at = pl.ds(c * TILE, TILE)
        return pltpu.make_async_copy(grad_hbm.at[:, at], grad.at[:, at], load_sem.at[c])

    def store(c):
        at = pl.ds(c * TILE, TILE)
        return pltpu.make_async_copy(total.at[:, at], out_hbm.at[:, at], store_sem.at[c])

    load_resid = pltpu.make_async_copy(resid_hbm, resid, load_sem.at[tiles])

    def load_disp(c):
        at = pl.ds(c * TILE, TILE)
        return pltpu.make_async_copy(disp_hbm.at[at], disp.at[at], load_sem.at[tiles + 1 + c])

    load_resid.start()
    for c in range(tiles):
        load_disp(c).start()
        load_grad(c).start()
    load_resid.wait()
    for c in range(tiles):
        at = pl.ds(c * TILE, TILE)
        load_disp(c).wait()
        term = lax.dot_general(resid[...], disp[at], (((1,), (1,)), ((), ())), preferred_element_type=jnp.float32)
        load_grad(c).wait()
        total[:, at] = (grad[:, at] + term) * (1.0 / 32.0)
        store(c).start()
    for c in range(tiles):
        store(c).wait()


def add_last(grad, resid, disp):
    anywhere = pl.BlockSpec(memory_space=pl.ANY)
    tiles = disp.shape[0] // TILE
    return pl.pallas_call(
        last_kernel,
        name="add_last",
        out_shape=jax.ShapeDtypeStruct(grad.shape, jnp.float32),
        in_specs=[anywhere] * 3,
        out_specs=anywhere,
        scratch_shapes=[
            pltpu.VMEM(grad.shape, jnp.float32),
            pltpu.VMEM(resid.shape, jnp.bfloat16),
            pltpu.VMEM(disp.shape, jnp.bfloat16),
            pltpu.VMEM(grad.shape, jnp.float32),
            pltpu.SemaphoreType.DMA((2 * tiles + 1,)),
            pltpu.SemaphoreType.DMA((tiles,)),
        ],
        compiler_params=pltpu.CompilerParams(vmem_limit_bytes=60 << 20),
    )(grad, resid, disp)


def local(eigvec, force_const, amplitudes, mlip_forces, frequency):
    return add_last(*exchange(eigvec.T, force_const, amplitudes, mlip_forces, frequency))


def solution(mesh):
    return jax.shard_map(
        local,
        mesh=mesh,
        in_specs=(
            P("row", ("col", "cfg")),
            P(("col", "cfg"), "row"),
            P(("col", "cfg"), None),
            P(("col", "cfg"), "row"),
            P(("col", "cfg")),
        ),
        out_specs=P(("col", "cfg"), "row"),
        check_vma=False,
    )
```
